32 devices in a mesh: dp: 8 (over z, x), space: 4 (over y, core).
Axes of the slice: x: 2, y: 2, z: 4, core: 2. Of those that a mesh axis runs over, the one named last changes fastest.
Arguments:
- latents: bfloat16 [48, 8, 32, 1280], P('dp', 'space'), may hold values from -42 to 42
- buckets: int32 [48, 2], P('dp'), may hold values from 6 to 32, as said below
- gn_gain: float32 [1280], replicated, may hold values from 0.1 to 1.9
- gn_shift: float32 [1280], replicated, may hold values from -3 to 3
- conv_weight: bfloat16 [9, 1280, 1280], P(None, 'dp'), may hold values from -0.0546875 to 0.0546875
- time_bias: float32 [48, 1280], P('dp'), may hold values from -5 to 5
Outputs:
- result: bfloat16 [48, 8, 32, 1280], P('dp', 'space')
The draws below stay inside these ranges and needn't reach their ends.
Inputs may be any that keep to these rules, and one draw needn't show every extreme that they name: `buckets`: column 0 is a frame's height, column 1 its width; heights are at least 6 and at most 8, widths at least 24 and at most 32; in every draw some frame has height 8 and width 32.
All inputs are finite; a program needn't handle non-finite values.
Results may differ from the reference program's by a relative error of at most 0.0035.
Values may be sent and summed in bfloat16 or wider, within the bound.
No kernel may reach another device: no remote copies, remote signals or barrier semaphores. Data moves between devices by JAX's collectives and lax.ppermute only.
A program may use at most 64 MiB of HBM per device.

```python
import math
import jax
import jax.numpy as jnp
from jax import lax

C = 1280
GROUPS = 32
W_MAX = 32
H_MAX = 8
FRAMES = 48


def draw_latents(key, part):
    keys = jax.random.split(key, 3)
    shape = (FRAMES, H_MAX, W_MAX, C)
    row_scale = jnp.exp(jax.random.uniform(keys[0], (FRAMES, H_MAX, 1, 1), jnp.float32, math.log(0.32), math.log(3.2)))
    col_scale = jnp.exp(jax.random.uniform(keys[1], (FRAMES, 1, W_MAX, 1), jnp.float32, math.log(0.32), math.log(3.2)))
    values = jnp.clip(jax.random.normal(keys[2], shape, jnp.float32), -4.0, 4.0) * row_scale * col_scale
    return values.astype(jnp.bfloat16)


def draw_buckets(key, part):
    keys = jax.random.split(key, 3)
    heights = jax.random.randint(keys[0], (FRAMES,), 3 * H_MAX // 4, H_MAX + 1, jnp.int32)
    widths = jax.random.randint(keys[1], (FRAMES,), 3 * W_MAX // 4, W_MAX + 1, jnp.int32)
    chosen = jax.random.randint(keys[2], (), 0, FRAMES, jnp.int32)
    picked = jnp.arange(FRAMES, dtype=jnp.int32) == chosen
    heights = jnp.where(picked, H_MAX, heights)
    widths = jnp.where(picked, W_MAX, widths)
    return jnp.stack([heights, widths], axis=1).astype(jnp.int32)


def level_of(own_key, extent, cuts, least, top_value):
    def one(position, parts):
        steps = jax.random.uniform(jax.random.fold_in(jax.random.fold_in(own_key, 6), position), (parts,), jnp.float32, least / len(cuts), top_value / len(cuts))
        return jnp.repeat(jnp.exp(steps), extent[position] // parts).reshape((-1,) + (1,) * (len(extent) - position - 1))

    level = one(*cuts[0])
    for cut in cuts[1:]:
        level = level * one(*cut)
    return level


def noise(rng, dims, width, bound, cuts=(), held_as=jnp.bfloat16):
    values = width * jax.random.normal(rng, dims, jnp.float32)
    if cuts:
        values = values * level_of(rng, dims, cuts, -0.22, 0.18)
    return jnp.clip(values, -bound, bound).astype(held_as)


def setup_inputs(seed: int = 0) -> dict:
    seeds = jax.random.split(jax.random.key(seed), 7)
    return {
        "latents": draw_latents(jax.random.fold_in(seeds[6], 71), 0),
        "buckets": draw_buckets(jax.random.fold_in(seeds[6], 71), 0),
        "gn_gain": jnp.clip(1.0 + 0.18 * jax.random.normal(seeds[2], (C,), jnp.float32), 0.1, 1.9),
        "gn_shift": noise(seeds[3], (C,), 0.5, 3.0, (), jnp.float32),
        "conv_weight": noise(seeds[4], (9, C, C), (9 * C) ** -0.5, 0.0546875, ((1, 8),)),
        "time_bias": noise(seeds[5], (FRAMES, C), 1.0, 5.0, ((0, 8),), jnp.float32),
    }


eps = 1e-05

def reference(latents, buckets, gn_gain, gn_shift, conv_weight, time_bias):
    height = latents.shape[1]
    width_cells = latents.shape[2]
    chans = latents.shape[3]
    members = chans // GROUPS
    row_ids = jnp.arange(height, dtype=jnp.int32)
    col_ids = jnp.arange(width_cells, dtype=jnp.int32)
    kernel = jnp.transpose(conv_weight.reshape(3, 3, chans, chans), (2, 0, 1, 3)).astype(jnp.float32)

    def frame_block(items):
        frame, sizes, bias_row = items
        valid = ((row_ids[:, None] < sizes[0]) & (col_ids[None, :] < sizes[1])).astype(jnp.float32)
        count = (sizes[0] * sizes[1]).astype(jnp.float32) * members
        values = frame.astype(jnp.float32).reshape(height, width_cells, GROUPS, members)
        weight_mask = valid[:, :, None, None]
        mean = lax.optimization_barrier(jnp.sum(values * weight_mask, axis=(0, 1, 3))) / count
        centered = values - mean[None, None, :, None]
        spread = lax.optimization_barrier(jnp.sum(centered * centered * weight_mask, axis=(0, 1, 3))) / count
        normed = (centered / jnp.sqrt(spread[None, None, :, None] + eps)).reshape(height, width_cells, chans)
        normed = normed * gn_gain + gn_shift
        act = (valid[:, :, None] * jax.nn.silu(normed)).astype(jnp.bfloat16)
        conv = lax.conv_general_dilated(act.astype(jnp.float32)[None], kernel, (1, 1), ((1, 1), (1, 1)), dimension_numbers=('NHWC', 'OHWI', 'NHWC'), precision=lax.Precision.HIGHEST)[0]
        conv_out = conv.astype(jnp.bfloat16)
        total = frame.astype(jnp.float32) + valid[:, :, None] * (conv_out.astype(jnp.float32) + bias_row)
        return total.astype(jnp.bfloat16)
    return lax.map(frame_block, (latents, buckets, time_bias))
```

```python
import jax
import jax.numpy as jnp
from jax import lax
from jax.sharding import PartitionSpec as P

GROUPS = 32
EPS = 1e-05
FRAME_BYTES = 8 << 20


def with_halo(x, sides, width):
    for axis, dim in sides:
        size, length = (lax.axis_size(axis), x.shape[dim])
        up = [(i, (i + 1) % size) for i in range(size - 1)]
        down = [(j, i) for i, j in up]
        last = lax.slice_in_dim(x, length - width, length, axis=dim)
        first = lax.slice_in_dim(x, 0, width, axis=dim)
        before = lax.ppermute(last, axis, up)
        after = lax.ppermute(first, axis, down)
        x = jnp.concatenate([before, x, after], axis=dim)
    return x


def tap_product(window, panel):
    return lax.dot_general(
        window, panel, (((3,), (1,)), ((), ())), preferred_element_type=jnp.float32
    )


def row_plan(latents, buckets, gn_gain, gn_shift, conv_weight, time_bias):
    frames, rows, cols, chans = latents.shape
    members = chans // GROUPS
    row_ids = lax.axis_index("space") * rows + jnp.arange(rows, dtype=jnp.int32)
    col_ids = jnp.arange(cols, dtype=jnp.int32)
    valid = (
        (row_ids[None, :, None] < buckets[:, 0][:, None, None])
        & (col_ids[None, None, :] < buckets[:, 1][:, None, None])
    ).astype(jnp.float32)
    count = (buckets[:, 0] * buckets[:, 1]).astype(jnp.float32)[:, None] * members
    values = latents.astype(jnp.float32).reshape(frames, rows, cols, GROUPS, members)
    weight_mask = valid[:, :, :, None, None]
    total = lax.psum(jnp.sum(values * weight_mask, axis=(1, 2, 4)), "space")
    mean = total / count
    centered = values - mean[:, None, None, :, None]
    spread = lax.psum(jnp.sum(centered * centered * weight_mask, axis=(1, 2, 4)), "space") / count
    normed = (centered / jnp.sqrt(spread[:, None, None, :, None] + EPS)).reshape(
        frames, rows, cols, chans
    )
    normed = normed * gn_gain + gn_shift
    act = (valid[..., None] * jax.nn.silu(normed)).astype(jnp.bfloat16)
    extended = with_halo(act, (("space", 1),), 1)
    padded = jnp.pad(extended, ((0, 0), (0, 0), (1, 1), (0, 0)))

    def add_tap(index, accum):
        window = lax.dynamic_slice(
            padded, (0, index // 3, index % 3, 0), (frames, rows, cols, chans)
        )
        panel = lax.dynamic_index_in_dim(conv_weight, index, 0, keepdims=False)
        return accum + tap_product(window, lax.all_gather(panel, "dp", axis=0, tiled=True))

    conv = lax.fori_loop(0, 9, add_tap, jnp.zeros((frames, rows, cols, chans), jnp.float32))
    conv_out = conv.astype(jnp.bfloat16)
    summed = latents.astype(jnp.float32) + valid[..., None] * (
        conv_out.astype(jnp.float32) + time_bias[:, None, None, :]
    )
    return summed.astype(jnp.bfloat16)


class Grid:
    def __init__(self, mesh):
        dp, space = mesh.shape["dp"], mesh.shape["space"]
        self.X = self.C = 2
        self.Z, self.Y = dp // 2, space // 2
        self.places = [
            (z, x, y, c)
            for z in range(self.Z)
            for x in range(2)
            for y in range(self.Y)
            for c in range(2)
        ]

    def linear(self, z, x, y, c):
        return ((z * 2 + x) * self.Y + y) * 2 + c

    def permute(self, value, target):
        pairs = []
        for place in self.places:
            goal = target(*place)
            if goal is not None:
                pairs.append((self.linear(*place), self.linear(*goal)))
        return lax.ppermute(value, ("dp", "space"), pairs)


def pick(flag, first, second):
    return jnp.where(flag == 0, first, second)


def by_source(grid, rounds, y, flip):
    ordered = []
    per_round = [
        [pick(flip, row[bit], row[1 - bit]) for bit in range(2)] for row in rounds
    ]
    for source in range(grid.Y):
        for bit in range(2):
            options = [per_round[i][bit] for i in range(grid.Y)]
            index = (y - source) % grid.Y
            ordered.append(lax.select_n(index, *options) if grid.Y > 2 else pick(index, *options))
    return ordered


def gather_line(grid, piece, z):
    Z = grid.Z
    below, above = [], []
    up = down = piece
    for step in range(1, Z):
        up = grid.permute(
            up, lambda z, x, y, c, s=step: (z + 1, x, y, c) if s - 1 <= z < Z - 1 else None
        )
        down = grid.permute(
            down, lambda z, x, y, c, s=step: (z - 1, x, y, c) if 1 <= z <= Z - s else None
        )
        below.append(up)
        above.append(down)
    pieces = []
    for source in range(Z):
        value = piece
        for step in range(1, Z):
            if source + step < Z:
                value = jnp.where(z == source + step, below[step - 1], value)
            if source - step >= 0:
                value = jnp.where(z == source - step, above[step - 1], value)
        pieces.append(value)
    return pieces


def on_device(grid, latents, buckets, gn_gain, gn_shift, conv_weight, time_bias):
    frames, rows, cols, chans = latents.shape
    members = chans // GROUPS
    taps, shard, _ = conv_weight.shape
    Y, Z = grid.Y, grid.Z
    part = shard // Y
    dp_index, space_index = lax.axis_index("dp"), lax.axis_index("space")
    z, x = dp_index // 2, dp_index % 2
    y, c = space_index // 2, space_index % 2

    rounds = [
        [
            grid.permute(latents, lambda z, x, y, c, i=i, j=j: (z, c ^ j, (y + i) % Y, x))
            for j in range(2)
        ]
        for i in range(Y)
    ]
    other_buckets = grid.permute(
        buckets, lambda z, x, y, c: (z, c, y, x)
    )
    mine = lax.dynamic_slice_in_dim(conv_weight, y * part, part, 1)
    half = chans // 2
    piece = lax.dynamic_slice_in_dim(mine, c * half, half, 2)
    pieces = gather_line(grid, piece, z)
    held = jnp.concatenate(pieces, axis=1)
    swapped = grid.permute(held, lambda z, x, y, c: (z, x, y, 1 - c))
    kernel = jnp.concatenate([pick(c, held, swapped), pick(c, swapped, held)], axis=2)

    full = jnp.concatenate(by_source(grid, rounds, y, x), axis=1)
    height = full.shape[1]
    row_ids = jnp.arange(height, dtype=jnp.int32)
    col_ids = jnp.arange(cols, dtype=jnp.int32)

    def valid_of(ids, sizes):
        return (
            (ids[None, :, None] < sizes[:, 0][:, None, None])
            & (col_ids[None, None, :] < sizes[:, 1][:, None, None])
        ).astype(jnp.float32)

    valid = valid_of(row_ids, other_buckets)
    count = (other_buckets[:, 0] * other_buckets[:, 1]).astype(jnp.float32)[:, None] * members
    values = full.astype(jnp.float32)
    mask = valid[..., None]

    def per_group(sums):
        grouped = jnp.sum(sums.reshape(frames, GROUPS, members), axis=2) / count
        return jnp.repeat(grouped, members, axis=1)[:, None, None, :]

    mean = per_group(jnp.sum(values * mask, axis=(1, 2)))
    centered = values - mean
    spread = per_group(jnp.sum(centered * centered * mask, axis=(1, 2)))
    normed = centered / jnp.sqrt(spread + EPS) * gn_gain + gn_shift
    act = (mask * jax.nn.silu(normed)).astype(jnp.bfloat16)

    conv = lax.conv_general_dilated(
        act,
        kernel.reshape(3, 3, Z * part, chans),
        (1, 1),
        ((1, 1), (1, 1)),
        dimension_numbers=("NHWC", "HWOI", "NHWC"),
        preferred_element_type=jnp.float32,
    ).astype(jnp.bfloat16)

    back = []
    for i in range(Y):
        row = []
        for j in range(2):
            first = rows * (((y + i) % Y) * 2 + (x ^ j))
            block = lax.dynamic_slice_in_dim(conv, first, rows, 1)
            row.append(
                grid.permute(block, lambda z, x, y, c, i=i, j=j: (z, c, (y + i) % Y, x ^ j))
            )
        back.append(row)
    parts = by_source(grid, back, y, c)
    stacked = jnp.stack(parts).reshape(Y, 2, frames, rows, cols, Z, part)
    conv_out = jnp.transpose(stacked, (2, 3, 4, 5, 1, 0, 6)).reshape(frames, rows, cols, chans)

    own_valid = valid_of(space_index * rows + jnp.arange(rows, dtype=jnp.int32), buckets)
    summed = latents.astype(jnp.float32) + own_valid[..., None] * (
        conv_out.astype(jnp.float32) + time_bias[:, None, None, :]
    )
    return summed.astype(jnp.bfloat16)


def solution(mesh):
    in_specs = (
        P("dp", "space", None, None),
        P("dp", None),
        P(),
        P(),
        P(None, "dp", None),
        P("dp", None),
    )
    grid = Grid(mesh)

    def body(latents, *rest):
        whole_frames = latents.size * latents.dtype.itemsize * mesh.shape["space"]
        if whole_frames > FRAME_BYTES:
            return row_plan(latents, *rest)
        return on_device(grid, latents, *rest)

    return jax.shard_map(
        body, mesh=mesh, in_specs=in_specs, out_specs=P("dp", "space", None, None), check_vma=False
    )
```

```python
import functools

import jax
import jax.numpy as jnp
from jax import lax
from jax.experimental import pallas as pl
from jax.experimental.pallas import tpu as pltpu
from jax.sharding import PartitionSpec as P

GROUPS = 32
EPS = 1e-05
FRAME_BYTES = 8 << 20


def with_halo(x, sides, width):
    for axis, dim in sides:
        size, length = (lax.axis_size(axis), x.shape[dim])
        up = [(i, (i + 1) % size) for i in range(size - 1)]
        down = [(j, i) for i, j in up]
        last = lax.slice_in_dim(x, length - width, length, axis=dim)
        first = lax.slice_in_dim(x, 0, width, axis=dim)
        before = lax.ppermute(last, axis, up)
        after = lax.ppermute(first, axis, down)
        x = jnp.concatenate([before, x, after], axis=dim)
    return x


def tap_product(window, panel):
    return lax.dot_general(
        window, panel, (((3,), (1,)), ((), ())), preferred_element_type=jnp.float32
    )


def row_plan(latents, buckets, gn_gain, gn_shift, conv_weight, time_bias):
    frames, rows, cols, chans = latents.shape
    members = chans // GROUPS
    row_ids = lax.axis_index("space") * rows + jnp.arange(rows, dtype=jnp.int32)
    col_ids = jnp.arange(cols, dtype=jnp.int32)
    valid = (
        (row_ids[None, :, None] < buckets[:, 0][:, None, None])
        & (col_ids[None, None, :] < buckets[:, 1][:, None, None])
    ).astype(jnp.float32)
    count = (buckets[:, 0] * buckets[:, 1]).astype(jnp.float32)[:, None] * members
    values = latents.astype(jnp.float32).reshape(frames, rows, cols, GROUPS, members)
    weight_mask = valid[:, :, :, None, None]
    total = lax.psum(jnp.sum(values * weight_mask, axis=(1, 2, 4)), "space")
    mean = total / count
    centered = values - mean[:, None, None, :, None]
    spread = lax.psum(jnp.sum(centered * centered * weight_mask, axis=(1, 2, 4)), "space") / count
    normed = (centered / jnp.sqrt(spread[:, None, None, :, None] + EPS)).reshape(
        frames, rows, cols, chans
    )
    normed = normed * gn_gain + gn_shift
    act = (valid[..., None] * jax.nn.silu(normed)).astype(jnp.bfloat16)
    extended = with_halo(act, (("space", 1),), 1)
    padded = jnp.pad(extended, ((0, 0), (0, 0), (1, 1), (0, 0)))

    def add_tap(index, accum):
        window = lax.dynamic_slice(
            padded, (0, index // 3, index % 3, 0), (frames, rows, cols, chans)
        )
        panel = lax.dynamic_index_in_dim(conv_weight, index, 0, keepdims=False)
        return accum + tap_product(window, lax.all_gather(panel, "dp", axis=0, tiled=True))

    conv = lax.fori_loop(0, 9, add_tap, jnp.zeros((frames, rows, cols, chans), jnp.float32))
    conv_out = conv.astype(jnp.bfloat16)
    summed = latents.astype(jnp.float32) + valid[..., None] * (
        conv_out.astype(jnp.float32) + time_bias[:, None, None, :]
    )
    return summed.astype(jnp.bfloat16)


class Grid:
    def __init__(self, mesh):
        dp, space = mesh.shape["dp"], mesh.shape["space"]
        self.X = self.C = 2
        self.Z, self.Y = dp // 2, space // 2
        self.places = [
            (z, x, y, c)
            for z in range(self.Z)
            for x in range(2)
            for y in range(self.Y)
            for c in range(2)
        ]

    def linear(self, z, x, y, c):
        return ((z * 2 + x) * self.Y + y) * 2 + c

    def permute(self, value, target):
        pairs = []
        for place in self.places:
            goal = target(*place)
            if goal is not None:
                pairs.append((self.linear(*place), self.linear(*goal)))
        return lax.ppermute(value, ("dp", "space"), pairs)


LANES = 128
ANY = pl.BlockSpec(memory_space=pl.ANY)
VMEM = pl.BlockSpec(memory_space=pltpu.VMEM)
SMEM = pl.BlockSpec(memory_space=pltpu.SMEM)


def params(mib):
    return pltpu.CompilerParams(vmem_limit_bytes=mib << 20)


def start_all(pairs, sems):
    copies = [pltpu.make_async_copy(src, dst, sems.at[n]) for n, (src, dst) in enumerate(pairs)]
    for copy in copies:
        copy.start()
    return copies


def piece_kernel(part, cuts, where, weight, *refs):
    outs, sems = refs[:-1], refs[-1]
    half = weight.shape[2] // 2
    rows = pl.ds(pl.multiple_of(where[2] * part, part), part)
    lanes = pl.ds(pl.multiple_of(where[3] * half, half), half)
    pairs = [
        (weight.at[pl.ds(first, count), rows, lanes], out)
        for (first, count), out in zip(cuts, outs)
    ]
    for copy in start_all(pairs, sems):
        copy.wait()


def own_pieces(where, weight, part, cuts):
    half = weight.shape[2] // 2
    return pl.pallas_call(
        functools.partial(piece_kernel, part, cuts),
        out_shape=[jax.ShapeDtypeStruct((n, part, half), weight.dtype) for _, n in cuts],
        in_specs=[SMEM, ANY],
        out_specs=[ANY] * len(cuts),
        scratch_shapes=[pltpu.SemaphoreType.DMA((len(cuts),))],
        compiler_params=params(4),
        cost_estimate=pl.CostEstimate(flops=0, transcendentals=0, bytes_accessed=4 << 20),
        name="own_pieces",
    )(where, weight)


def exact_dot(value, ones):
    total = None
    for _ in range(3):
        top = value.astype(jnp.bfloat16)
        term = jnp.dot(top, ones, preferred_element_type=jnp.float32)
        total = term if total is None else total + term
        value = value - top.astype(jnp.float32)
    return total


def act_kernel(begin, where, sizes, gain, shift, group, group_t, *refs):
    rounds, act, sums, scale = refs[:4], refs[4], refs[5], refs[6]
    frames, rows, cols, chans = rounds[0].shape
    members = chans // GROUPS
    x, y = where[1], where[2]
    tiles = chans // LANES
    first_row = [rows * (2 * (y ^ (k // 2)) + (x ^ (k % 2))) for k in range(4)]
    col_ids = lax.broadcasted_iota(jnp.int32, (cols, LANES), 0)

    def limit(f, k, r):
        return jnp.where(first_row[k] + r < sizes[begin + f, 0], sizes[begin + f, 1], 0)

    def fold(v):
        return jnp.sum(v.reshape(cols // 8, 8, LANES), axis=0)

    def keep(kind, value):
        for f in range(frames):
            scale[8 * kind + f] = value[f : f + 1]

    sums[...] = jnp.zeros_like(sums)

    def add_sums(f, _):
        masks = [[col_ids < limit(f, k, r) for r in range(rows)] for k in range(4)]
        for t in range(tiles):
            lanes = slice(t * LANES, (t + 1) * LANES)
            total = jnp.zeros((8, LANES), jnp.float32)
            for k in range(4):
                for r in range(rows):
                    v = rounds[k][f, r, :, lanes].astype(jnp.float32)
                    total += fold(jnp.where(masks[k][r], v, 0.0))
            sums[f, :, lanes] = total
        return 0

    lax.fori_loop(0, frames, add_sums, 0)
    ids = lax.broadcasted_iota(jnp.int32, (8, LANES), 0)
    count = jnp.ones((8, LANES), jnp.float32)
    for f in range(frames):
        cells = (sizes[begin + f, 0] * sizes[begin + f, 1] * members).astype(jnp.float32)
        count = jnp.where(ids == f, cells, count)
    mean = exact_dot(jnp.sum(sums[...], axis=1), group[...]) / count
    keep(0, exact_dot(mean, group_t[...]))

    def add_squares(f, _):
        masks = [[col_ids < limit(f, k, r) for r in range(rows)] for k in range(4)]
        for t in range(tiles):
            lanes = slice(t * LANES, (t + 1) * LANES)
            middle = scale[f, :, lanes]
            total = jnp.zeros((8, LANES), jnp.float32)
            for k in range(4):
                for r in range(rows):
                    v = rounds[k][f, r, :, lanes].astype(jnp.float32) - middle
                    total += fold(jnp.where(masks[k][r], v * v, 0.0))
            sums[f, :, lanes] = total
        return 0

    lax.fori_loop(0, frames, add_squares, 0)
    spread = exact_dot(jnp.sum(sums[...], axis=1), group[...]) / count
    keep(1, exact_dot(1.0 / jnp.sqrt(spread + EPS), group_t[...]) * gain[...])

    def activate(f, _):
        for t in range(tiles):
            lanes = slice(t * LANES, (t + 1) * LANES)
            middle = scale[f, :, lanes]
            factor = scale[8 + f, :, lanes]
            offset = shift[:, lanes]
            for k in range(4):
                for r in range(rows):
                    v = rounds[k][f, r, :, lanes].astype(jnp.float32)
                    v = (v - middle) * factor + offset
                    v = v / (1.0 + jnp.exp(-v))
                    v = jnp.where(col_ids < limit(f, k, r), v, 0.0)
                    act[first_row[k] + r + 1, f, :, lanes] = v.astype(jnp.bfloat16)
        return 0

    lax.fori_loop(0, frames, activate, 0)
    edge = jnp.zeros((frames, cols, chans), jnp.bfloat16)
    act[0] = edge
    act[act.shape[0] - 1] = edge


def group_matrix(chans):
    member = jnp.arange(chans, dtype=jnp.int32)[:, None] // (chans // GROUPS)
    return (member == jnp.arange(LANES, dtype=jnp.int32)[None, :]).astype(jnp.bfloat16)


def activation(where, sizes, gain, shift, group, rounds, begin):
    frames, rows, cols, chans = rounds[0].shape
    elements = 4 * rounds[0].size
    return pl.pallas_call(
        functools.partial(act_kernel, begin),
        out_shape=jax.ShapeDtypeStruct((4 * rows + 2, frames, cols, chans), jnp.bfloat16),
        in_specs=[SMEM, SMEM] + [VMEM] * 8,
        out_specs=VMEM,
        scratch_shapes=[
            pltpu.VMEM((8, 8, chans), jnp.float32),
            pltpu.VMEM((16, 1, chans), jnp.float32),
        ],
        compiler_params=params(8),
        cost_estimate=pl.CostEstimate(
            flops=2 * elements, transcendentals=0, bytes_accessed=elements
        ),
        name="activation",
    )(where, sizes, gain[None, :], shift[None, :], *group, *rounds)


def shifted_sum(left, middle, right, cols):
    size = middle.shape[0]
    col = lax.broadcasted_iota(jnp.int32, middle.shape, 0) % cols
    left = jnp.where(col == 0, 0.0, pltpu.roll(left, 1, 0))
    right = jnp.where(col == cols - 1, 0.0, pltpu.roll(right, size - 1, 0))
    return middle + left + right


def conv_rows(act, weight, first_tap, taps, base, chunk, line, cols):
    columns = []
    for dc in range(3):
        total = None
        for dr in range(3):
            tap = 3 * dr + dc - first_tap
            if not 0 <= tap < taps:
                continue
            window = act[pl.ds(pl.multiple_of(base + dr * line, cols), chunk), :]
            term = lax.dot_general(
                window,
                weight[tap],
                (((1,), (1,)), ((), ())),
                preferred_element_type=jnp.float32,
            )
            total = term if total is None else total + term
        columns.append(total)
    return shifted_sum(*columns, cols)


def conv_kernel(rows, cols, part, first_tap, counts, halves, own_taps, more, where, *refs):
    takes_sums, gives_sums, unread = more
    z, x, y, c = (where[n] for n in range(4))
    acts, refs = refs[:halves], refs[halves:]
    own, refs = (refs[0], refs[1:]) if own_taps else (None, refs)
    given, refs = refs[: 2 * len(counts)], refs[2 * len(counts) :]
    sums_in, refs = (refs[:halves], refs[halves:]) if takes_sums else (None, refs)
    refs = refs[unread:]
    outs, refs = refs[: halves if gives_sums else 4], refs[halves if gives_sums else 4 :]
    weight, refs = refs[0], refs[1:]
    results, sems = refs[:-1], refs[-1]
    half = weight.shape[2] // 2
    taps, width = weight.shape[0], weight.shape[1]
    pairs = []
    if own_taps:
        low = jnp.where(z < 2, 0, 1)
        places = [
            jnp.where(z == 0, 1, z - 1) - low,
            jnp.where(z < 3, 2, 0),
        ]
        pairs.append(
            (
                own.at[
                    pl.ds(first_tap, own_taps), pl.ds(pl.multiple_of(y * part, part), part), :
                ],
                weight.at[:, pl.ds(pl.multiple_of((z - low) * part, part), part), :],
            )
        )
    else:
        places = [0]
    for n, (tap, size, slot) in enumerate(counts):
        goal = pl.ds(pl.multiple_of(places[slot] * part, part), part)
        for m, side in enumerate((c, 1 - c)):
            lanes = pl.ds(pl.multiple_of(side * half, half), half)
            pairs.append((given[2 * n + m], weight.at[pl.ds(tap, size), goal, lanes]))
    for copy in start_all(pairs, sems):
        copy.wait()
    for n, act in enumerate(acts):
        frames = act.shape[0] // (10 * cols) if act.shape[0] % (10 * cols) == 0 else 0
        line = frames * cols
        size = act.shape[0] - 2 * line
        chunk = size // 2

        def body(m, _, act=act, n=n, frames=frames, line=line, chunk=chunk):
            base = pl.multiple_of(m * chunk, chunk)
            value = conv_rows(act, weight, first_tap, taps, base, chunk, line, cols)
            if takes_sums:
                value += sums_in[n][pl.ds(base, chunk), :]
            if gives_sums:
                outs[n][pl.ds(base, chunk), :] = value
            else:
                value = value.astype(jnp.bfloat16).reshape(chunk // line, frames, cols, width)
                results[n][pl.ds(m * (chunk // line), chunk // line)] = value
            return 0

        lax.fori_loop(0, size // chunk, body, 0)
    if gives_sums:
        return
    for k, out in enumerate(outs):
        first = rows * (2 * (y ^ (k // 2)) + (x ^ (k % 2)))
        for n, result in enumerate(results):
            frames = result.shape[1]
            out[:, n * frames : (n + 1) * frames, :, 0:width] = result[pl.ds(first, rows)]
        if out.shape[3] > width:
            blank = out.shape[:3] + (out.shape[3] - width,)
            out[:, :, :, width:] = jnp.zeros(blank, out.dtype)


def convolution(
    where, acts, own, given, counts, first_tap, taps, slots, part, rows, sums=None, ends=True, after=()
):
    padded, frames, cols, chans = acts[0].shape
    height = padded - 2
    width = part * slots
    lanes = -(-width // LANES) * LANES
    halves = len(acts)
    if ends:
        out = jax.ShapeDtypeStruct((rows, frames * halves, cols, lanes), jnp.bfloat16)
        out_shape = [out] * 4
        results = [pltpu.VMEM((height, frames, cols, width), jnp.bfloat16)] * halves
    else:
        out_shape = [jax.ShapeDtypeStruct((height * frames * cols, width), jnp.float32)] * halves
        results = []
    operands = [act.reshape(padded * frames * cols, chans) for act in acts]
    specs = [VMEM] * halves
    if own is not None:
        operands.append(own)
        specs.append(ANY)
    operands += given
    specs += [ANY] * len(given)
    if sums is not None:
        operands += sums
        specs += [VMEM] * halves
    operands += after
    specs += [ANY] * len(after)
    return pl.pallas_call(
        functools.partial(
            conv_kernel,
            rows,
            cols,
            part,
            first_tap,
            counts,
            halves,
            taps if own is not None else 0,
            (sums is not None, not ends, len(after)),
        ),
        out_shape=out_shape,
        in_specs=[SMEM] + specs,
        out_specs=[VMEM] * len(out_shape),
        scratch_shapes=[pltpu.VMEM((taps, width, chans), jnp.bfloat16)]
        + results
        + [pltpu.SemaphoreType.DMA((len(given) + 1,))],
        compiler_params=params(24),
        cost_estimate=pl.CostEstimate(
            flops=2 * height * frames * cols * taps * chans * 256,
            transcendentals=0,
            bytes_accessed=taps * width * chans * 2,
        ),
        name="convolution",
    )(where, *operands)


def result_kernel(where, sizes, latents, bias, *refs):
    main, last, out = refs[:4], refs[4:8], refs[8]
    main_buf, last_buf, sems = refs[9:]
    frames, rows, cols, chans = latents.shape
    part = chans // 16
    z, y, c = where[0], where[2], where[3]
    pairs = []
    for k in range(4):
        place = 2 * (c ^ (k % 2)) + (y ^ (k // 2))
        pairs.append((main[k], main_buf.at[place]))
        pairs.append((last[k], last_buf.at[place]))
    for copy in start_all(pairs, sems):
        copy.wait()
    first_row = rows * (2 * y + c)
    col_ids = lax.broadcasted_iota(jnp.int32, (cols, chans), 0)

    def finish(low):
        def body(f, _):
            for r in range(rows):
                chunks = []
                for shard in range(4):
                    for q in range(4):
                        if low <= shard < low + 3:
                            lanes = slice((shard - low) * part, (shard - low + 1) * part)
                            chunk = main_buf[q, r, f, :, lanes]
                        else:
                            chunk = last_buf[q, r, f, :, 0:part]
                        chunks.append(chunk.astype(jnp.float32))
                value = jnp.concatenate(chunks, axis=1) + bias[f]
                limit = jnp.where(first_row + r < sizes[f, 0], sizes[f, 1], 0)
                value = latents[f, r].astype(jnp.float32) + jnp.where(col_ids < limit, value, 0.0)
                out[f, r] = value.astype(jnp.bfloat16)
            return 0

        lax.fori_loop(0, frames, body, 0)

    @pl.when(z < 2)
    def _():
        finish(0)

    @pl.when(z >= 2)
    def _():
        finish(1)


def final_result(where, sizes, latents, bias, main, last):
    return pl.pallas_call(
        result_kernel,
        out_shape=jax.ShapeDtypeStruct(latents.shape, latents.dtype),
        in_specs=[SMEM, SMEM, VMEM, VMEM] + [ANY] * 8,
        out_specs=VMEM,
        scratch_shapes=[
            pltpu.VMEM((4,) + main[0].shape, jnp.bfloat16),
            pltpu.VMEM((4,) + last[0].shape, jnp.bfloat16),
            pltpu.SemaphoreType.DMA((8,)),
        ],
        compiler_params=params(12),
        cost_estimate=pl.CostEstimate(
            flops=4 * latents.size, transcendentals=0, bytes_accessed=8 * latents.size
        ),
        name="final_result",
    )(where, sizes, latents, bias[:, None, :], *main, *last)


def frame_plan(grid, latents, buckets, gn_gain, gn_shift, conv_weight, time_bias):
    frames, rows, cols, chans = latents.shape
    taps = conv_weight.shape[0]
    part = conv_weight.shape[1] // 2
    early, late = 6, taps - 6
    dp_index, space_index = lax.axis_index("dp"), lax.axis_index("space")
    z, x = dp_index // 2, dp_index % 2
    y, c = space_index // 2, space_index % 2
    where = jnp.stack([z, x, y, c]).astype(jnp.int32)

    def spread(values):
        return [
            grid.permute(v, lambda z, x, y, c, k=k: (z, c, y ^ (k // 2), x ^ (k % 2)))
            for k, v in enumerate(values)
        ]

    def spread_in(value):
        return [
            grid.permute(value, lambda z, x, y, c, k=k: (z, c ^ (k % 2), y ^ (k // 2), x))
            for k in range(4)
        ]

    def up(value, first):
        return grid.permute(value, lambda z, x, y, c: (z + 1, x, y, c) if first <= z < 3 else None)

    def down(value, last):
        return grid.permute(value, lambda z, x, y, c: (z - 1, x, y, c) if 1 <= z <= last else None)

    def swap(value):
        return grid.permute(value, lambda z, x, y, c: (z, x, y, 1 - c))

    group = group_matrix(chans)
    group = (group, group.T)
    half = frames // 2

    (piece,) = own_pieces(where, conv_weight, part, ((0, taps),))
    sizes = grid.permute(buckets, lambda z, x, y, c: (z, c, y, x))
    up1, down1 = up(piece, 0), down(piece, 3)
    rounds0 = spread_in(latents[:half])
    rest = latents[half:]
    up1, down1, rounds0, rest = lax.optimization_barrier((up1, down1, rounds0, rest))

    up2, down2 = up(up1, 1), down(down1, 2)
    rounds1 = spread_in(rest)
    slot1 = jnp.where(z == 0, down1, up1)
    slot1_other = swap(slot1)
    act0 = activation(where, sizes, gn_gain, gn_shift, group, rounds0, 0)
    up2, down2, rounds1, act0, slot1, slot1_other = lax.optimization_barrier(
        (up2, down2, rounds1, act0, slot1, slot1_other)
    )

    near = lax.optimization_barrier((up2, down2, up1, down1))
    up3 = [up(up2[:early], 2), up(up2[early:], 2)]
    down3 = [down(down2[:early], 1), down(down2[early:], 1)]
    slot2 = jnp.where(z == 0, near[1], jnp.where(z == 3, near[0], near[3]))
    slot2_other = swap(slot2)
    act1 = activation(where, sizes, gn_gain, gn_shift, group, rounds1, half)
    acts = [act0, act1]
    main = convolution(
        where,
        acts,
        conv_weight,
        [slot1, slot1_other, slot2, slot2_other],
        ((0, taps, 0), (0, taps, 1)),
        0,
        taps,
        3,
        part,
        rows,
    )

    def pick_last(n, taken):
        a, b, c_, d = taken
        return jnp.where(z < 2, jnp.where(z == 0, a, b), jnp.where(z == 2, c_, d))

    first_cut, second_cut = slice(0, early), slice(early, taps)
    taken = lax.optimization_barrier((down3[0], down2[first_cut], up2[first_cut], up3[0], main))
    slot3 = pick_last(0, taken[:4])
    sums = convolution(
        where,
        acts,
        None,
        [slot3, swap(slot3)],
        ((0, early, 0),),
        0,
        early,
        1,
        part,
        rows,
        ends=False,
        after=taken[4][:1],
    )
    taken = lax.optimization_barrier((down3[1], down2[second_cut], up2[second_cut], up3[1]))
    slot3 = pick_last(1, taken)
    last = convolution(
        where,
        acts,
        None,
        [slot3, swap(slot3)],
        ((0, late, 0),),
        early,
        late,
        1,
        part,
        rows,
        sums=sums,
    )
    return final_result(where, buckets, latents, time_bias, spread(main), spread(last))


def solution(mesh):
    in_specs = (
        P("dp", "space", None, None),
        P("dp", None),
        P(),
        P(),
        P(None, "dp", None),
        P("dp", None),
    )
    grid = Grid(mesh)

    def body(latents, *rest):
        if (grid.Z, grid.Y) == (4, 2) and latents.shape[1] == 2:
            return frame_plan(grid, latents, *rest)
        return row_plan(latents, *rest)

    return jax.shard_map(
        body, mesh=mesh, in_specs=in_specs, out_specs=P("dp", "space", None, None), check_vma=False
    )
```

```python
import functools

import jax
import jax.numpy as jnp
from jax import lax
from jax.experimental import pallas as pl
from jax.experimental.pallas import tpu as pltpu
from jax.sharding import PartitionSpec as P

GROUPS = 32
EPS = 1e-05
FRAME_BYTES = 8 << 20


def with_halo(x, sides, width):
    for axis, dim in sides:
        size, length = (lax.axis_size(axis), x.shape[dim])
        up = [(i, (i + 1) % size) for i in range(size - 1)]
        down = [(j, i) for i, j in up]
        last = lax.slice_in_dim(x, length - width, length, axis=dim)
        first = lax.slice_in_dim(x, 0, width, axis=dim)
        before = lax.ppermute(last, axis, up)
        after = lax.ppermute(first, axis, down)
        x = jnp.concatenate([before, x, after], axis=dim)
    return x


def tap_product(window, panel):
    return lax.dot_general(
        window, panel, (((3,), (1,)), ((), ())), preferred_element_type=jnp.float32
    )


def row_plan(latents, buckets, gn_gain, gn_shift, conv_weight, time_bias):
    frames, rows, cols, chans = latents.shape
    members = chans // GROUPS
    row_ids = lax.axis_index("space") * rows + jnp.arange(rows, dtype=jnp.int32)
    col_ids = jnp.arange(cols, dtype=jnp.int32)
    valid = (
        (row_ids[None, :, None] < buckets[:, 0][:, None, None])
        & (col_ids[None, None, :] < buckets[:, 1][:, None, None])
    ).astype(jnp.float32)
    count = (buckets[:, 0] * buckets[:, 1]).astype(jnp.float32)[:, None] * members
    values = latents.astype(jnp.float32).reshape(frames, rows, cols, GROUPS, members)
    weight_mask = valid[:, :, :, None, None]
    total = lax.psum(jnp.sum(values * weight_mask, axis=(1, 2, 4)), "space")
    mean = total / count
    centered = values - mean[:, None, None, :, None]
    spread = lax.psum(jnp.sum(centered * centered * weight_mask, axis=(1, 2, 4)), "space") / count
    normed = (centered / jnp.sqrt(spread[:, None, None, :, None] + EPS)).reshape(
        frames, rows, cols, chans
    )
    normed = normed * gn_gain + gn_shift
    act = (valid[..., None] * jax.nn.silu(normed)).astype(jnp.bfloat16)
    extended = with_halo(act, (("space", 1),), 1)
    padded = jnp.pad(extended, ((0, 0), (0, 0), (1, 1), (0, 0)))

    def add_tap(index, accum):
        window = lax.dynamic_slice(
            padded, (0, index // 3, index % 3, 0), (frames, rows, cols, chans)
        )
        panel = lax.dynamic_index_in_dim(conv_weight, index, 0, keepdims=False)
        return accum + tap_product(window, lax.all_gather(panel, "dp", axis=0, tiled=True))

    conv = lax.fori_loop(0, 9, add_tap, jnp.zeros((frames, rows, cols, chans), jnp.float32))
    conv_out = conv.astype(jnp.bfloat16)
    summed = latents.astype(jnp.float32) + valid[..., None] * (
        conv_out.astype(jnp.float32) + time_bias[:, None, None, :]
    )
    return summed.astype(jnp.bfloat16)


class Grid:
    def __init__(self, mesh):
        dp, space = mesh.shape["dp"], mesh.shape["space"]
        self.X = self.C = 2
        self.Z, self.Y = dp // 2, space // 2
        self.places = [
            (z, x, y, c)
            for z in range(self.Z)
            for x in range(2)
            for y in range(self.Y)
            for c in range(2)
        ]

    def linear(self, z, x, y, c):
        return ((z * 2 + x) * self.Y + y) * 2 + c

    def permute(self, value, target):
        pairs = []
        for place in self.places:
            goal = target(*place)
            if goal is not None:
                pairs.append((self.linear(*place), self.linear(*goal)))
        return lax.ppermute(value, ("dp", "space"), pairs)


LANES = 128
ANY = pl.BlockSpec(memory_space=pl.ANY)
VMEM = pl.BlockSpec(memory_space=pltpu.VMEM)
SMEM = pl.BlockSpec(memory_space=pltpu.SMEM)


def params(mib):
    return pltpu.CompilerParams(vmem_limit_bytes=mib << 20)


def start_all(pairs, sems):
    copies = [pltpu.make_async_copy(src, dst, sems.at[n]) for n, (src, dst) in enumerate(pairs)]
    for copy in copies:
        copy.start()
    return copies


def piece_kernel(part, where, weight, out, sem):
    rows = pl.ds(pl.multiple_of(where[2] * part, part), part)
    copy = pltpu.make_async_copy(weight.at[:, rows, :], out, sem.at[0])
    copy.start()
    copy.wait()


def own_piece(where, weight, part):
    taps, _, chans = weight.shape
    return pl.pallas_call(
        functools.partial(piece_kernel, part),
        out_shape=jax.ShapeDtypeStruct((taps, part, chans), weight.dtype),
        in_specs=[SMEM, ANY],
        out_specs=ANY,
        scratch_shapes=[pltpu.SemaphoreType.DMA((1,))],
        compiler_params=params(56),
        cost_estimate=pl.CostEstimate(flops=0, transcendentals=0, bytes_accessed=4 << 20),
        name="own_piece",
    )(where, weight)


def choose(index, sources, target, sem, wait):
    for value, source in enumerate(sources):

        @pl.when(index == value)
        def _(source=source):
            copy = pltpu.make_async_copy(source, target, sem)
            copy.wait() if wait else copy.start()


def exact_dot(value, ones):
    total = None
    for _ in range(3):
        top = value.astype(jnp.bfloat16)
        term = jnp.dot(top, ones, preferred_element_type=jnp.float32)
        total = term if total is None else total + term
        value = value - top.astype(jnp.float32)
    return total


def act_kernel(begin, where, sizes, gain, shift, group, group_t, *refs):
    given, act, blocks, sums, scale, sems = refs[:6], *refs[6:]
    frames, rows, cols, chans = blocks.shape[1:]
    members = chans // GROUPS
    x, y, c = where[1], where[2], where[3]
    span = pl.ds(begin, frames)
    away = jnp.where(c == x, 0, 1)
    same0, same1, other0, other1, relay0, relay1 = (ref.at[span] for ref in given)
    choices = [(same0, same0), (same1, same1), (other0, relay0), (other1, relay1)]
    for wait in (False, True):
        for k, pair in enumerate(choices):
            choose(away, pair, blocks.at[k], sems.at[k], wait)
    tiles = chans // LANES
    first_row = [rows * (2 * (y ^ (k // 2)) + (x ^ (k % 2))) for k in range(4)]
    col_ids = lax.broadcasted_iota(jnp.int32, (cols, LANES), 0)

    def limit(f, k, r):
        return jnp.where(first_row[k] + r < sizes[begin + f, 0], sizes[begin + f, 1], 0)

    def fold(v):
        return jnp.sum(v.reshape(cols // 8, 8, LANES), axis=0)

    def keep(kind, value):
        for f in range(frames):
            scale[8 * kind + f] = value[f : f + 1]

    sums[...] = jnp.zeros_like(sums)

    def add_sums(f, _):
        masks = [[col_ids < limit(f, k, r) for r in range(rows)] for k in range(4)]
        for t in range(tiles):
            lanes = slice(t * LANES, (t + 1) * LANES)
            total = jnp.zeros((8, LANES), jnp.float32)
            for k in range(4):
                for r in range(rows):
                    v = blocks[k, f, r, :, lanes].astype(jnp.float32)
                    total += fold(jnp.where(masks[k][r], v, 0.0))
            sums[f, :, lanes] = total
        return 0

    lax.fori_loop(0, frames, add_sums, 0)
    ids = lax.broadcasted_iota(jnp.int32, (8, LANES), 0)
    count = jnp.ones((8, LANES), jnp.float32)
    for f in range(frames):
        cells = (sizes[begin + f, 0] * sizes[begin + f, 1] * members).astype(jnp.float32)
        count = jnp.where(ids == f, cells, count)
    mean = exact_dot(jnp.sum(sums[...], axis=1), group[...]) / count
    keep(0, exact_dot(mean, group_t[...]))

    def add_squares(f, _):
        masks = [[col_ids < limit(f, k, r) for r in range(rows)] for k in range(4)]
        for t in range(tiles):
            lanes = slice(t * LANES, (t + 1) * LANES)
            middle = scale[f, :, lanes]
            total = jnp.zeros((8, LANES), jnp.float32)
            for k in range(4):
                for r in range(rows):
                    v = blocks[k, f, r, :, lanes].astype(jnp.float32) - middle
                    total += fold(jnp.where(masks[k][r], v * v, 0.0))
            sums[f, :, lanes] = total
        return 0

    lax.fori_loop(0, frames, add_squares, 0)
    spread = exact_dot(jnp.sum(sums[...], axis=1), group[...]) / count
    keep(1, exact_dot(1.0 / jnp.sqrt(spread + EPS), group_t[...]) * gain[...])

    def activate(f, _):
        for t in range(tiles):
            lanes = slice(t * LANES, (t + 1) * LANES)
            middle = scale[f, :, lanes]
            factor = scale[8 + f, :, lanes]
            offset = shift[:, lanes]
            for k in range(4):
                for r in range(rows):
                    v = blocks[k, f, r, :, lanes].astype(jnp.float32)
                    v = (v - middle) * factor + offset
                    v = v / (1.0 + jnp.exp(-v))
                    v = jnp.where(col_ids < limit(f, k, r), v, 0.0)
                    act[first_row[k] + r + 1, f, :, lanes] = v.astype(jnp.bfloat16)
        return 0

    lax.fori_loop(0, frames, activate, 0)
    edge = jnp.zeros((frames, cols, chans), jnp.bfloat16)
    act[0] = edge
    act[act.shape[0] - 1] = edge


def group_matrix(chans):
    member = jnp.arange(chans, dtype=jnp.int32)[:, None] // (chans // GROUPS)
    return (member == jnp.arange(LANES, dtype=jnp.int32)[None, :]).astype(jnp.bfloat16)


def activation(where, sizes, gain, shift, group, blocks, begin, frames):
    _, rows, cols, chans = blocks[0].shape
    elements = 4 * frames * rows * cols * chans
    return pl.pallas_call(
        functools.partial(act_kernel, begin),
        out_shape=jax.ShapeDtypeStruct((4 * rows + 2, frames, cols, chans), jnp.bfloat16),
        in_specs=[SMEM, SMEM] + [VMEM] * 4 + [ANY] * 6,
        out_specs=VMEM,
        scratch_shapes=[
            pltpu.VMEM((4, frames, rows, cols, chans), jnp.bfloat16),
            pltpu.VMEM((8, 8, chans), jnp.float32),
            pltpu.VMEM((16, 1, chans), jnp.float32),
            pltpu.SemaphoreType.DMA((4,)),
        ],
        compiler_params=params(12),
        cost_estimate=pl.CostEstimate(
            flops=2 * elements, transcendentals=0, bytes_accessed=elements
        ),
        name="activation",
    )(where, sizes, gain[None, :], shift[None, :], *group, *blocks)


def shifted_sum(left, middle, right, cols):
    size = middle.shape[0]
    col = lax.broadcasted_iota(jnp.int32, middle.shape, 0) % cols
    left = jnp.where(col == 0, 0.0, pltpu.roll(left, 1, 0))
    right = jnp.where(col == cols - 1, 0.0, pltpu.roll(right, size - 1, 0))
    return middle + left + right


def window(act, base, dr, chunk, line, cols):
    return act[pl.ds(pl.multiple_of(base + dr * line, cols), chunk), :]


def product(rows, weight):
    return lax.dot_general(
        rows, weight, (((1,), (1,)), ((), ())), preferred_element_type=jnp.float32
    )


def give_rows(where, results, outs, rows):
    x, y = where[1], where[2]
    for k, out in enumerate(outs):
        first = rows * (2 * (y ^ (k // 2)) + (x ^ (k % 2)))
        width = results[0].shape[3]
        for n, result in enumerate(results):
            frames = result.shape[1]
            out[:, n * frames : (n + 1) * frames, :, 0:width] = result[pl.ds(first, rows)]
        if out.shape[3] > width:
            blank = out.shape[:3] + (out.shape[3] - width,)
            out[:, :, :, width:] = jnp.zeros(blank, out.dtype)


def all_rows(acts, results, cols, compute):
    for act, result in zip(acts, results):
        frames = result.shape[1]
        line = frames * cols
        chunk = result.shape[0] * line // 2
        lines = chunk // line

        def body(m, _, act=act, result=result, frames=frames, line=line, chunk=chunk, lines=lines):
            base = pl.multiple_of(m * chunk, chunk)
            value = compute(act, base, chunk, line).astype(jnp.bfloat16)
            result[pl.ds(m * lines, lines)] = value.reshape(lines, frames, cols, value.shape[1])
            return 0

        lax.fori_loop(0, 2, body, 0)


def from_below(hop, c):
    return 2 * hop + c


def from_above(hop, c):
    return 2 * hop + 1 - c


def main_kernel(rows, cols, part, where, act0, act1, own, *refs):
    z, y, c = where[0], where[2], where[3]
    hops, refs = refs[:4], refs[4:]
    outs, weight, results, sems = refs[:4], refs[4], refs[5:7], refs[7]
    low = jnp.where(z < 2, 0, 1)

    def rows_of(place):
        return pl.ds(pl.multiple_of(place * part, part), part)

    mine = pltpu.make_async_copy(own, weight.at[:, rows_of(z - low), :], sems.at[2])
    mine.start()
    first = jnp.where(z == 0, from_above(0, c), from_below(0, c))
    second = jnp.where(
        z == 0, from_above(1, c), jnp.where(z == 3, from_below(1, c), from_above(0, c))
    )
    first_rows = rows_of(jnp.where(z == 0, 1, z - 1) - low)
    second_rows = rows_of(jnp.where(z < 3, 2, 0))
    for wait in (False, True):
        choose(first, hops[:2], weight.at[:, first_rows, :], sems.at[0], wait)
        choose(second, hops, weight.at[:, second_rows, :], sems.at[1], wait)
    mine.wait()

    def compute(act, base, chunk, line):
        columns = []
        for dc in range(3):
            total = None
            for dr in range(3):
                term = product(window(act, base, dr, chunk, line, cols), weight[3 * dr + dc])
                total = term if total is None else total + term
            columns.append(total)
        return shifted_sum(*columns, cols)

    all_rows((act0, act1), results, cols, compute)
    give_rows(where, results, outs, rows)


def last_kernel(rows, cols, part, where, act0, act1, *refs):
    z, c = where[0], where[3]
    hops, refs = refs[:4], refs[4:]
    outs, weight, results, sems = refs[:4], refs[4], refs[5:7], refs[7]
    index = jnp.where(
        z < 2,
        jnp.where(z == 0, from_above(1, c), from_above(0, c)),
        jnp.where(z == 2, from_below(0, c), from_below(1, c)),
    )
    for wait in (False, True):
        choose(index, hops, weight, sems.at[0], wait)

    def compute(act, base, chunk, line):
        total = None
        for dr in range(3):
            taps = weight[3 * dr : 3 * dr + 3].reshape(3 * part, weight.shape[2])
            term = product(window(act, base, dr, chunk, line, cols), taps)
            total = term if total is None else total + term
        columns = [total[:, dc * part : (dc + 1) * part] for dc in range(3)]
        return shifted_sum(*columns, cols)

    all_rows((act0, act1), results, cols, compute)
    give_rows(where, results, outs, rows)


def convolution(kernel, where, acts, weights, part, rows, shards):
    padded, frames, cols, chans = acts[0].shape
    height = padded - 2
    width = part * shards
    lanes = -(-width // LANES) * LANES
    out = jax.ShapeDtypeStruct((rows, 2 * frames, cols, lanes), jnp.bfloat16)
    return pl.pallas_call(
        functools.partial(kernel, rows, cols, part),
        out_shape=[out] * 4,
        in_specs=[SMEM, VMEM, VMEM] + [ANY] * len(weights),
        out_specs=[VMEM] * 4,
        scratch_shapes=[
            pltpu.VMEM((9, width, chans), jnp.bfloat16),
            pltpu.VMEM((height, frames, cols, width), jnp.bfloat16),
            pltpu.VMEM((height, frames, cols, width), jnp.bfloat16),
            pltpu.SemaphoreType.DMA((3,)),
        ],
        compiler_params=params(24),
        cost_estimate=pl.CostEstimate(
            flops=4 * height * frames * cols * 9 * chans * width,
            transcendentals=0,
            bytes_accessed=9 * width * chans * 2,
        ),
        name="convolution",
    )(where, *[act.reshape(padded * frames * cols, chans) for act in acts], *weights)


def place_of(where, k):
    return 2 * (where[3] ^ (k % 2)) + (where[2] ^ (k // 2))


def bring(where, parts, buffer, sems):
    copies = [
        pltpu.make_async_copy(part, buffer.at[place_of(where, k)], sems.at[k])
        for k, part in enumerate(parts)
    ]
    for copy in copies:
        copy.start()
    for copy in copies:
        copy.wait()


def main_result_kernel(where, sizes, latents, bias, *refs):
    parts, out, buffer, sems = refs[:4], *refs[4:]
    frames, rows, cols, chans = latents.shape
    part = chans // 16
    bring(where, parts, buffer, sems)
    first_row = rows * (2 * where[2] + where[3])
    col_ids = lax.broadcasted_iota(jnp.int32, (cols, 12 * part), 0)

    def finish(low):
        lanes = slice(low * 4 * part, (low + 3) * 4 * part)
        rest = slice(12 * part, chans) if low == 0 else slice(0, 4 * part)

        def body(f, _):
            for r in range(rows):
                chunks = [
                    buffer[q, r, f, :, n * part : (n + 1) * part].astype(jnp.float32)
                    for n in range(3)
                    for q in range(4)
                ]
                value = jnp.concatenate(chunks, axis=1) + bias[f, :, lanes]
                limit = jnp.where(first_row + r < sizes[f, 0], sizes[f, 1], 0)
                value = jnp.where(col_ids < limit, value, 0.0)
                value += latents[f, r, :, lanes].astype(jnp.float32)
                out[f, r, :, lanes] = value.astype(jnp.bfloat16)
                out[f, r, :, rest] = latents[f, r, :, rest]
            return 0

        lax.fori_loop(0, frames, body, 0)

    for low in (0, 1):
        pl.when((where[0] >= 2) == bool(low))(functools.partial(finish, low))


def main_result(where, sizes, latents, bias, parts):
    return pl.pallas_call(
        main_result_kernel,
        out_shape=jax.ShapeDtypeStruct(latents.shape, latents.dtype),
        in_specs=[SMEM, SMEM, VMEM, VMEM] + [ANY] * 4,
        out_specs=VMEM,
        scratch_shapes=[
            pltpu.VMEM((4,) + parts[0].shape, jnp.bfloat16),
            pltpu.SemaphoreType.DMA((4,)),
        ],
        compiler_params=params(12),
        cost_estimate=pl.CostEstimate(
            flops=4 * latents.size, transcendentals=0, bytes_accessed=4 * latents.size
        ),
        name="main_result",
    )(where, sizes, latents, bias, *parts)


def last_result_kernel(where, sizes, bias, given, *refs):
    parts, out, buffer, slab, sems = refs[:4], *refs[4:]
    del given
    frames, rows, cols, wide = slab.shape
    chans = out.shape[3]
    part = chans // 16
    first_row = rows * (2 * where[2] + where[3])
    col_ids = lax.broadcasted_iota(jnp.int32, (cols, 4 * part), 0)

    def finish(low):
        begin = 0 if low else chans - wide
        inner = slice(0, 4 * part) if low else slice(wide - 4 * part, wide)
        lanes = slice(0, 4 * part) if low else slice(chans - 4 * part, chans)
        home = out.at[:, :, :, begin : begin + wide]
        copy = pltpu.make_async_copy(home, slab, sems.at[4])
        copy.start()
        bring(where, parts, buffer, sems)
        copy.wait()

        def body(f, _):
            for r in range(rows):
                chunks = [buffer[q, r, f, :, 0:part].astype(jnp.float32) for q in range(4)]
                value = jnp.concatenate(chunks, axis=1) + bias[f, :, lanes]
                limit = jnp.where(first_row + r < sizes[f, 0], sizes[f, 1], 0)
                value = jnp.where(col_ids < limit, value, 0.0)
                value += slab[f, r, :, inner].astype(jnp.float32)
                slab[f, r, :, inner] = value.astype(jnp.bfloat16)
            return 0

        lax.fori_loop(0, frames, body, 0)
        copy = pltpu.make_async_copy(slab, home, sems.at[4])
        copy.start()
        copy.wait()

    for low in (0, 1):
        pl.when((where[0] >= 2) == bool(low))(functools.partial(finish, low))


def last_result(where, sizes, bias, given, parts):
    frames, rows, cols, chans = given.shape
    wide = -(-(chans // 4) // LANES) * LANES
    return pl.pallas_call(
        last_result_kernel,
        out_shape=jax.ShapeDtypeStruct(given.shape, given.dtype),
        in_specs=[SMEM, SMEM, VMEM, ANY] + [ANY] * 4,
        out_specs=ANY,
        scratch_shapes=[
            pltpu.VMEM((4,) + parts[0].shape, jnp.bfloat16),
            pltpu.VMEM((frames, rows, cols, wide), jnp.bfloat16),
            pltpu.SemaphoreType.DMA((5,)),
        ],
        input_output_aliases={3: 0},
        compiler_params=params(8),
        cost_estimate=pl.CostEstimate(
            flops=given.size, transcendentals=0, bytes_accessed=given.size
        ),
        name="last_result",
    )(where, sizes, bias, given, *parts)


def frame_plan(grid, latents, buckets, gn_gain, gn_shift, conv_weight, time_bias):
    frames, rows, cols, chans = latents.shape
    part = conv_weight.shape[1] // 2
    dp_index, space_index = lax.axis_index("dp"), lax.axis_index("space")
    z, x = dp_index // 2, dp_index % 2
    y, c = space_index // 2, space_index % 2
    where = jnp.stack([z, x, y, c]).astype(jnp.int32)

    def spread(values):
        return [
            grid.permute(v, lambda z, x, y, c, k=k: (z, c, y ^ (k // 2), x ^ (k % 2)))
            for k, v in enumerate(values)
        ]

    def hop(value, step):
        def target(z, x, y, c):
            if c == 0:
                return (z + 1, x, y, c) if step - 1 <= z < 3 else None
            return (z - 1, x, y, c) if 1 <= z <= 4 - step else None

        return grid.permute(value, target)

    def swap(value):
        return grid.permute(value, lambda z, x, y, c: (z, x, y, 1 - c))

    def same_y(j):
        return grid.permute(latents, lambda z, x, y, c: (z, c ^ j, y, x))

    def other_y(j):
        return grid.permute(latents, lambda z, x, y, c: (z, x, 1 - y, x) if c == x ^ j else None)

    group = group_matrix(chans)
    group = (group, group.T)
    half = frames // 2

    piece = own_piece(where, conv_weight, part)
    hop1 = hop(piece, 1)
    blocks = [same_y(0), same_y(1), other_y(0), other_y(1)]
    hop1, blocks, buckets = lax.optimization_barrier((hop1, blocks, buckets))

    hop2 = hop(hop1, 2)
    relay0 = grid.permute(blocks[0], lambda z, x, y, c: (z, x, 1 - y, c) if c != x else None)
    relay1 = grid.permute(blocks[2], lambda z, x, y, c: (z, 1 - x, y, c) if c == x else None)
    sizes = grid.permute(buckets, lambda z, x, y, c: (z, c, y, x))
    blocks += [relay0, relay1]
    swap1 = swap(hop1)
    act0 = activation(where, sizes, gn_gain, gn_shift, group, blocks, 0, half)
    hop2, blocks, act0, swap1 = lax.optimization_barrier((hop2, blocks, act0, swap1))

    hop3 = hop(hop2, 3)
    swap2 = swap(hop2)
    act1 = activation(where, sizes, gn_gain, gn_shift, group, blocks, half, half)
    acts = [act0, act1]
    weights = [piece, hop1, swap1, hop2, swap2]
    main = convolution(main_kernel, where, acts, weights, part, rows, 3)

    hop3, main = lax.optimization_barrier((hop3, main))
    weights = [hop2, swap2, hop3, swap(hop3)]
    last = convolution(last_kernel, where, acts, weights, part, rows, 1)
    bias = time_bias[:, None, :]
    result = main_result(where, buckets, latents, bias, spread(main))
    return last_result(where, buckets, bias, result, spread(last))


def solution(mesh):
    in_specs = (
        P("dp", "space", None, None),
        P("dp", None),
        P(),
        P(),
        P(None, "dp", None),
        P("dp", None),
    )
    grid = Grid(mesh)

    def body(latents, *rest):
        if (grid.Z, grid.Y) == (4, 2) and latents.shape[1] == 2:
            return frame_plan(grid, latents, *rest)
        return row_plan(latents, *rest)

    return jax.shard_map(
        body, mesh=mesh, in_specs=in_specs, out_specs=P("dp", "space", None, None), check_vma=False
    )
```

```python
import functools

import jax
import jax.numpy as jnp
from jax import lax
from jax.experimental import pallas as pl
from jax.experimental.pallas import tpu as pltpu
from jax.sharding import PartitionSpec as P

GROUPS = 32
EPS = 1e-05
FRAME_BYTES = 8 << 20


def with_halo(x, sides, width):
    for axis, dim in sides:
        size, length = (lax.axis_size(axis), x.shape[dim])
        up = [(i, (i + 1) % size) for i in range(size - 1)]
        down = [(j, i) for i, j in up]
        last = lax.slice_in_dim(x, length - width, length, axis=dim)
        first = lax.slice_in_dim(x, 0, width, axis=dim)
        before = lax.ppermute(last, axis, up)
        after = lax.ppermute(first, axis, down)
        x = jnp.concatenate([before, x, after], axis=dim)
    return x


def tap_product(window, panel):
    return lax.dot_general(
        window, panel, (((3,), (1,)), ((), ())), preferred_element_type=jnp.float32
    )


def row_plan(latents, buckets, gn_gain, gn_shift, conv_weight, time_bias):
    frames, rows, cols, chans = latents.shape
    members = chans // GROUPS
    row_ids = lax.axis_index("space") * rows + jnp.arange(rows, dtype=jnp.int32)
    col_ids = jnp.arange(cols, dtype=jnp.int32)
    valid = (
        (row_ids[None, :, None] < buckets[:, 0][:, None, None])
        & (col_ids[None, None, :] < buckets[:, 1][:, None, None])
    ).astype(jnp.float32)
    count = (buckets[:, 0] * buckets[:, 1]).astype(jnp.float32)[:, None] * members
    values = latents.astype(jnp.float32).reshape(frames, rows, cols, GROUPS, members)
    weight_mask = valid[:, :, :, None, None]
    total = lax.psum(jnp.sum(values * weight_mask, axis=(1, 2, 4)), "space")
    mean = total / count
    centered = values - mean[:, None, None, :, None]
    spread = lax.psum(jnp.sum(centered * centered * weight_mask, axis=(1, 2, 4)), "space") / count
    normed = (centered / jnp.sqrt(spread[:, None, None, :, None] + EPS)).reshape(
        frames, rows, cols, chans
    )
    normed = normed * gn_gain + gn_shift
    act = (valid[..., None] * jax.nn.silu(normed)).astype(jnp.bfloat16)
    extended = with_halo(act, (("space", 1),), 1)
    padded = jnp.pad(extended, ((0, 0), (0, 0), (1, 1), (0, 0)))

    def add_tap(index, accum):
        window = lax.dynamic_slice(
            padded, (0, index // 3, index % 3, 0), (frames, rows, cols, chans)
        )
        panel = lax.dynamic_index_in_dim(conv_weight, index, 0, keepdims=False)
        return accum + tap_product(window, lax.all_gather(panel, "dp", axis=0, tiled=True))

    conv = lax.fori_loop(0, 9, add_tap, jnp.zeros((frames, rows, cols, chans), jnp.float32))
    conv_out = conv.astype(jnp.bfloat16)
    summed = latents.astype(jnp.float32) + valid[..., None] * (
        conv_out.astype(jnp.float32) + time_bias[:, None, None, :]
    )
    return summed.astype(jnp.bfloat16)


class Grid:
    def __init__(self, mesh):
        dp, space = mesh.shape["dp"], mesh.shape["space"]
        self.X = self.C = 2
        self.Z, self.Y = dp // 2, space // 2
        self.places = [
            (z, x, y, c)
            for z in range(self.Z)
            for x in range(2)
            for y in range(self.Y)
            for c in range(2)
        ]

    def linear(self, z, x, y, c):
        return ((z * 2 + x) * self.Y + y) * 2 + c

    def permute(self, value, target):
        pairs = []
        for place in self.places:
            goal = target(*place)
            if goal is not None:
                pairs.append((self.linear(*place), self.linear(*goal)))
        return lax.ppermute(value, ("dp", "space"), pairs)


LANES = 128
ANY = pl.BlockSpec(memory_space=pl.ANY)
VMEM = pl.BlockSpec(memory_space=pltpu.VMEM)
SMEM = pl.BlockSpec(memory_space=pltpu.SMEM)


def params(mib):
    return pltpu.CompilerParams(vmem_limit_bytes=mib << 20)


def start_all(pairs, sems):
    copies = [pltpu.make_async_copy(src, dst, sems.at[n]) for n, (src, dst) in enumerate(pairs)]
    for copy in copies:
        copy.start()
    return copies


def piece_kernel(part, where, weight, *refs):
    outs, sems = refs[:-1], refs[-1]
    rows = pl.ds(pl.multiple_of(where[2] * part, part), part)
    first, copies = 0, []
    for n, out in enumerate(outs):
        taps = pl.ds(first, out.shape[0])
        copies.append(pltpu.make_async_copy(weight.at[taps, rows, :], out, sems.at[n]))
        first += out.shape[0]
    for copy in copies:
        copy.start()
    for copy in copies:
        copy.wait()


def own_pieces(where, weight, part, cuts):
    chans = weight.shape[2]
    return pl.pallas_call(
        functools.partial(piece_kernel, part),
        out_shape=[jax.ShapeDtypeStruct((n, part, chans), weight.dtype) for n in cuts],
        in_specs=[SMEM, ANY],
        out_specs=[VMEM] * len(cuts),
        scratch_shapes=[pltpu.SemaphoreType.DMA((len(cuts),))],
        compiler_params=params(56),
        cost_estimate=pl.CostEstimate(flops=0, transcendentals=0, bytes_accessed=4 << 20),
        name="own_pieces",
    )(where, weight)


def choose(index, sources, target, sem, wait):
    for value, source in enumerate(sources):

        @pl.when(index == value)
        def _(source=source):
            copy = pltpu.make_async_copy(source, target, sem)
            copy.wait() if wait else copy.start()


def exact_dot(value, ones):
    total = None
    for _ in range(3):
        top = value.astype(jnp.bfloat16)
        term = jnp.dot(top, ones, preferred_element_type=jnp.float32)
        total = term if total is None else total + term
        value = value - top.astype(jnp.float32)
    return total


def act_kernel(begin, where, sizes, gain, shift, group, group_t, *refs):
    given, act, blocks, sums, scale, sems = refs[:6], *refs[6:]
    frames, rows, cols, chans = blocks.shape[1:]
    members = chans // GROUPS
    x, y, c = where[1], where[2], where[3]
    span = pl.ds(begin, frames)
    away = jnp.where(c == x, 0, 1)
    same0, same1, other0, other1, relay0, relay1 = (ref.at[span] for ref in given)
    choices = [(same0, same0), (same1, same1), (other0, relay0), (other1, relay1)]
    for wait in (False, True):
        for k, pair in enumerate(choices):
            choose(away, pair, blocks.at[k], sems.at[k], wait)
    tiles = chans // LANES
    first_row = [rows * (2 * (y ^ (k // 2)) + (x ^ (k % 2))) for k in range(4)]
    col_ids = lax.broadcasted_iota(jnp.int32, (cols, LANES), 0)

    def limit(f, k, r):
        return jnp.where(first_row[k] + r < sizes[begin + f, 0], sizes[begin + f, 1], 0)

    def fold(v):
        return jnp.sum(v.reshape(cols // 8, 8, LANES), axis=0)

    def keep(kind, value):
        for f in range(frames):
            scale[8 * kind + f] = value[f : f + 1]

    sums[...] = jnp.zeros_like(sums)

    def add_sums(f, _):
        masks = [[col_ids < limit(f, k, r) for r in range(rows)] for k in range(4)]
        for t in range(tiles):
            lanes = slice(t * LANES, (t + 1) * LANES)
            total = jnp.zeros((8, LANES), jnp.float32)
            for k in range(4):
                for r in range(rows):
                    v = blocks[k, f, r, :, lanes].astype(jnp.float32)
                    total += fold(jnp.where(masks[k][r], v, 0.0))
            sums[f, :, lanes] = total
        return 0

    lax.fori_loop(0, frames, add_sums, 0)
    ids = lax.broadcasted_iota(jnp.int32, (8, LANES), 0)
    count = jnp.ones((8, LANES), jnp.float32)
    for f in range(frames):
        cells = (sizes[begin + f, 0] * sizes[begin + f, 1] * members).astype(jnp.float32)
        count = jnp.where(ids == f, cells, count)
    mean = exact_dot(jnp.sum(sums[...], axis=1), group[...]) / count
    keep(0, exact_dot(mean, group_t[...]))

    def add_squares(f, _):
        masks = [[col_ids < limit(f, k, r) for r in range(rows)] for k in range(4)]
        for t in range(tiles):
            lanes = slice(t * LANES, (t + 1) * LANES)
            middle = scale[f, :, lanes]
            total = jnp.zeros((8, LANES), jnp.float32)
            for k in range(4):
                for r in range(rows):
                    v = blocks[k, f, r, :, lanes].astype(jnp.float32) - middle
                    total += fold(jnp.where(masks[k][r], v * v, 0.0))
            sums[f, :, lanes] = total
        return 0

    lax.fori_loop(0, frames, add_squares, 0)
    spread = exact_dot(jnp.sum(sums[...], axis=1), group[...]) / count
    keep(1, exact_dot(1.0 / jnp.sqrt(spread + EPS), group_t[...]) * gain[...])

    def activate(f, _):
        for t in range(tiles):
            lanes = slice(t * LANES, (t + 1) * LANES)
            middle = scale[f, :, lanes]
            factor = scale[8 + f, :, lanes]
            offset = shift[:, lanes]
            for k in range(4):
                for r in range(rows):
                    v = blocks[k, f, r, :, lanes].astype(jnp.float32)
                    v = (v - middle) * factor + offset
                    v = v / (1.0 + jnp.exp(-v))
                    v = jnp.where(col_ids < limit(f, k, r), v, 0.0)
                    act[first_row[k] + r + 1, f, :, lanes] = v.astype(jnp.bfloat16)
        return 0

    lax.fori_loop(0, frames, activate, 0)
    edge = jnp.zeros((frames, cols, chans), jnp.bfloat16)
    act[0] = edge
    act[act.shape[0] - 1] = edge


def group_matrix(chans):
    member = jnp.arange(chans, dtype=jnp.int32)[:, None] // (chans // GROUPS)
    return (member == jnp.arange(LANES, dtype=jnp.int32)[None, :]).astype(jnp.bfloat16)


def activation(where, sizes, gain, shift, group, blocks, begin, frames):
    _, rows, cols, chans = blocks[0].shape
    elements = 4 * frames * rows * cols * chans
    return pl.pallas_call(
        functools.partial(act_kernel, begin),
        out_shape=jax.ShapeDtypeStruct((4 * rows + 2, frames, cols, chans), jnp.bfloat16),
        in_specs=[SMEM, SMEM] + [VMEM] * 4 + [ANY] * 6,
        out_specs=VMEM,
        scratch_shapes=[
            pltpu.VMEM((4, frames, rows, cols, chans), jnp.bfloat16),
            pltpu.VMEM((8, 8, chans), jnp.float32),
            pltpu.VMEM((16, 1, chans), jnp.float32),
            pltpu.SemaphoreType.DMA((4,)),
        ],
        compiler_params=params(12),
        cost_estimate=pl.CostEstimate(
            flops=2 * elements, transcendentals=0, bytes_accessed=elements
        ),
        name="activation",
    )(where, sizes, gain[None, :], shift[None, :], *group, *blocks)


def shifted_sum(left, middle, right, cols):
    size = middle.shape[0]
    col = lax.broadcasted_iota(jnp.int32, middle.shape, 0) % cols
    left = jnp.where(col == 0, 0.0, pltpu.roll(left, 1, 0))
    right = jnp.where(col == cols - 1, 0.0, pltpu.roll(right, size - 1, 0))
    return middle + left + right


def window(act, base, dr, chunk, line, cols):
    return act[pl.ds(pl.multiple_of(base + dr * line, cols), chunk), :]


def product(rows, weight):
    return lax.dot_general(
        rows, weight, (((1,), (1,)), ((), ())), preferred_element_type=jnp.float32
    )


def give_rows(where, results, outs, rows):
    x, y = where[1], where[2]
    for k, out in enumerate(outs):
        first = rows * (2 * (y ^ (k // 2)) + (x ^ (k % 2)))
        width = results[0].shape[3]
        for n, result in enumerate(results):
            frames = result.shape[1]
            out[:, n * frames : (n + 1) * frames, :, 0:width] = result[pl.ds(first, rows)]
        if out.shape[3] > width:
            blank = out.shape[:3] + (out.shape[3] - width,)
            out[:, :, :, width:] = jnp.zeros(blank, out.dtype)


def all_rows(acts, results, cols, compute):
    for act, result in zip(acts, results):
        frames = result.shape[1]
        line = frames * cols
        chunk = result.shape[0] * line // 2
        lines = chunk // line

        def body(m, _, act=act, result=result, frames=frames, line=line, chunk=chunk, lines=lines):
            base = pl.multiple_of(m * chunk, chunk)
            value = compute(act, base, chunk, line).astype(jnp.bfloat16)
            result[pl.ds(m * lines, lines)] = value.reshape(lines, frames, cols, value.shape[1])
            return 0

        lax.fori_loop(0, 2, body, 0)


def from_below(hop, c):
    return 2 * hop + c


def from_above(hop, c):
    return 2 * hop + 1 - c


def main_kernel(rows, cols, part, where, act0, act1, *refs):
    z, c = where[0], where[3]
    own, hops, refs = refs[:2], (refs[2:6], refs[6:10]), refs[10:]
    outs, weight, results, sems = refs[:4], refs[4], refs[5:7], refs[7]
    low = jnp.where(z < 2, 0, 1)

    def rows_of(place):
        return pl.ds(pl.multiple_of(place * part, part), part)

    first = jnp.where(z == 0, from_above(0, c), from_below(0, c))
    second = jnp.where(
        z == 0, from_above(1, c), jnp.where(z == 3, from_below(1, c), from_above(0, c))
    )
    first_rows = rows_of(jnp.where(z == 0, 1, z - 1) - low)
    second_rows = rows_of(jnp.where(z < 3, 2, 0))
    for wait in (False, True):
        tap = 0
        for n in range(2):
            taps = pl.ds(tap, own[n].shape[0])
            tap += own[n].shape[0]
            mine = weight.at[taps, rows_of(z - low), :]
            choose(0, own[n : n + 1], mine, sems.at[3 * n], wait)
            choose(first, hops[n][:2], weight.at[taps, first_rows, :], sems.at[3 * n + 1], wait)
            choose(second, hops[n], weight.at[taps, second_rows, :], sems.at[3 * n + 2], wait)

    def compute(act, base, chunk, line):
        columns = []
        for dc in range(3):
            total = None
            for dr in range(3):
                term = product(window(act, base, dr, chunk, line, cols), weight[3 * dr + dc])
                total = term if total is None else total + term
            columns.append(total)
        return shifted_sum(*columns, cols)

    all_rows((act0, act1), results, cols, compute)
    give_rows(where, results, outs, rows)


def farthest(where):
    z, c = where[0], where[3]
    return jnp.where(
        z < 2,
        jnp.where(z == 0, from_above(1, c), from_above(0, c)),
        jnp.where(z == 2, from_below(0, c), from_below(1, c)),
    )


def tap_rows(act, weight, part, base, chunk, line, cols, first):
    total = None
    for n in range(weight.shape[0] // 3):
        taps = weight[3 * n : 3 * n + 3].reshape(3 * part, weight.shape[2])
        term = product(window(act, base, first + n, chunk, line, cols), taps)
        total = term if total is None else total + term
    return total


def last_kernel(rows, cols, part, where, act0, act1, *refs):
    hops, refs = (refs[:4], refs[4:8]), refs[8:]
    outs, weight, results, sems = refs[:4], refs[4], refs[5:7], refs[7]
    for wait in (False, True):
        tap = 0
        for n in range(2):
            taps = pl.ds(tap, hops[n][0].shape[0])
            tap += hops[n][0].shape[0]
            choose(farthest(where), hops[n], weight.at[taps], sems.at[n], wait)

    def compute(act, base, chunk, line):
        total = tap_rows(act, weight, part, base, chunk, line, cols, 0)
        columns = [total[:, dc * part : (dc + 1) * part] for dc in range(3)]
        return shifted_sum(*columns, cols)

    all_rows((act0, act1), results, cols, compute)
    give_rows(where, results, outs, rows)


def convolution(kernel, where, acts, weights, part, rows, shards):
    padded, frames, cols, chans = acts[0].shape
    height = padded - 2
    taps, width = 9, part * shards
    lanes = -(-width // LANES) * LANES
    out = jax.ShapeDtypeStruct((rows, 2 * frames, cols, lanes), jnp.bfloat16)
    return pl.pallas_call(
        functools.partial(kernel, rows, cols, part),
        out_shape=[out] * 4,
        in_specs=[SMEM, VMEM, VMEM] + [ANY] * len(weights),
        out_specs=[VMEM] * 4,
        scratch_shapes=[
            pltpu.VMEM((taps, width, chans), jnp.bfloat16),
            pltpu.VMEM((height, frames, cols, width), jnp.bfloat16),
            pltpu.VMEM((height, frames, cols, width), jnp.bfloat16),
            pltpu.SemaphoreType.DMA((6,)),
        ],
        compiler_params=params(6 + 2 * taps),
        cost_estimate=pl.CostEstimate(
            flops=4 * height * frames * cols * taps * chans * width,
            transcendentals=0,
            bytes_accessed=taps * width * chans * 2,
        ),
        name="convolution",
    )(where, *[act.reshape(padded * frames * cols, chans) for act in acts], *weights)


def place_of(where, k):
    return 2 * (where[3] ^ (k % 2)) + (where[2] ^ (k // 2))


def bring(where, parts, buffer, sems):
    copies = [
        pltpu.make_async_copy(part, buffer.at[place_of(where, k)], sems.at[k])
        for k, part in enumerate(parts)
    ]
    for copy in copies:
        copy.start()
    for copy in copies:
        copy.wait()


def main_result_kernel(where, sizes, latents, bias, *refs):
    parts, out, buffer, sems = refs[:4], *refs[4:]
    frames, rows, cols, chans = latents.shape
    part = chans // 16
    bring(where, parts, buffer, sems)
    first_row = rows * (2 * where[2] + where[3])
    col_ids = lax.broadcasted_iota(jnp.int32, (cols, 12 * part), 0)

    def finish(low):
        lanes = slice(low * 4 * part, (low + 3) * 4 * part)
        rest = slice(12 * part, chans) if low == 0 else slice(0, 4 * part)

        def body(f, _):
            for r in range(rows):
                chunks = [
                    buffer[q, r, f, :, n * part : (n + 1) * part].astype(jnp.float32)
                    for n in range(3)
                    for q in range(4)
                ]
                value = jnp.concatenate(chunks, axis=1) + bias[f, :, lanes]
                limit = jnp.where(first_row + r < sizes[f, 0], sizes[f, 1], 0)
                value = jnp.where(col_ids < limit, value, 0.0)
                value += latents[f, r, :, lanes].astype(jnp.float32)
                out[f, r, :, lanes] = value.astype(jnp.bfloat16)
                out[f, r, :, rest] = latents[f, r, :, rest]
            return 0

        lax.fori_loop(0, frames, body, 0)

    for low in (0, 1):
        pl.when((where[0] >= 2) == bool(low))(functools.partial(finish, low))


def main_result(where, sizes, latents, bias, parts):
    return pl.pallas_call(
        main_result_kernel,
        out_shape=jax.ShapeDtypeStruct(latents.shape, latents.dtype),
        in_specs=[SMEM, SMEM, VMEM, VMEM] + [ANY] * 4,
        out_specs=VMEM,
        scratch_shapes=[
            pltpu.VMEM((4,) + parts[0].shape, jnp.bfloat16),
            pltpu.SemaphoreType.DMA((4,)),
        ],
        compiler_params=params(12),
        cost_estimate=pl.CostEstimate(
            flops=4 * latents.size, transcendentals=0, bytes_accessed=4 * latents.size
        ),
        name="main_result",
    )(where, sizes, latents, bias, *parts)


def last_result_kernel(where, sizes, bias, given, *refs):
    parts, out, buffer, slab, sems = refs[:4], *refs[4:]
    del given
    frames, rows, cols, wide = slab.shape
    chans = out.shape[3]
    part = chans // 16
    first_row = rows * (2 * where[2] + where[3])
    col_ids = lax.broadcasted_iota(jnp.int32, (cols, 4 * part), 0)

    def finish(low):
        begin = 0 if low else chans - wide
        inner = slice(0, 4 * part) if low else slice(wide - 4 * part, wide)
        lanes = slice(0, 4 * part) if low else slice(chans - 4 * part, chans)
        home = out.at[:, :, :, begin : begin + wide]
        copy = pltpu.make_async_copy(home, slab, sems.at[4])
        copy.start()
        bring(where, parts, buffer, sems)
        copy.wait()

        def body(f, _):
            for r in range(rows):
                chunks = [buffer[q, r, f, :, 0:part].astype(jnp.float32) for q in range(4)]
                value = jnp.concatenate(chunks, axis=1) + bias[f, :, lanes]
                limit = jnp.where(first_row + r < sizes[f, 0], sizes[f, 1], 0)
                value = jnp.where(col_ids < limit, value, 0.0)
                value += slab[f, r, :, inner].astype(jnp.float32)
                slab[f, r, :, inner] = value.astype(jnp.bfloat16)
            return 0

        lax.fori_loop(0, frames, body, 0)
        copy = pltpu.make_async_copy(slab, home, sems.at[4])
        copy.start()
        copy.wait()

    for low in (0, 1):
        pl.when((where[0] >= 2) == bool(low))(functools.partial(finish, low))


def last_result(where, sizes, bias, given, parts):
    frames, rows, cols, chans = given.shape
    wide = -(-(chans // 4) // LANES) * LANES
    return pl.pallas_call(
        last_result_kernel,
        out_shape=jax.ShapeDtypeStruct(given.shape, given.dtype),
        in_specs=[SMEM, SMEM, VMEM, ANY] + [ANY] * 4,
        out_specs=ANY,
        scratch_shapes=[
            pltpu.VMEM((4,) + parts[0].shape, jnp.bfloat16),
            pltpu.VMEM((frames, rows, cols, wide), jnp.bfloat16),
            pltpu.SemaphoreType.DMA((5,)),
        ],
        input_output_aliases={3: 0},
        compiler_params=params(8),
        cost_estimate=pl.CostEstimate(
            flops=given.size, transcendentals=0, bytes_accessed=given.size
        ),
        name="last_result",
    )(where, sizes, bias, given, *parts)


def frame_plan(grid, latents, buckets, gn_gain, gn_shift, conv_weight, time_bias):
    frames, rows, cols, chans = latents.shape
    part = conv_weight.shape[1] // 2
    dp_index, space_index = lax.axis_index("dp"), lax.axis_index("space")
    z, x = dp_index // 2, dp_index % 2
    y, c = space_index // 2, space_index % 2
    where = jnp.stack([z, x, y, c]).astype(jnp.int32)

    def spread(values):
        return [
            grid.permute(v, lambda z, x, y, c, k=k: (z, c, y ^ (k // 2), x ^ (k % 2)))
            for k, v in enumerate(values)
        ]

    def hop(value, step):
        def target(z, x, y, c):
            if c == 0:
                return (z + 1, x, y, c) if step - 1 <= z < 3 else None
            return (z - 1, x, y, c) if 1 <= z <= 4 - step else None

        return grid.permute(value, target)

    def swap(value):
        return grid.permute(value, lambda z, x, y, c: (z, x, y, 1 - c))

    def same_y(j):
        return grid.permute(latents, lambda z, x, y, c: (z, c ^ j, y, x))

    def other_y(j):
        return grid.permute(latents, lambda z, x, y, c: (z, x, 1 - y, x) if c == x ^ j else None)

    group = group_matrix(chans)
    group = (group, group.T)
    half = frames // 2

    cuts = (6, conv_weight.shape[0] - 6)
    pieces = own_pieces(where, conv_weight, part, cuts)
    hop1 = [hop(pieces[0], 1), None]
    blocks = [same_y(0), same_y(1), other_y(0), other_y(1)]
    hop1[0], later = lax.optimization_barrier((hop1[0], pieces[1]))
    hop1[1] = hop(later, 1)
    swap1 = [swap(hop1[0]), None]
    hop2 = [hop(hop1[0], 2), None]
    hop1[1], blocks, buckets = lax.optimization_barrier((hop1[1], blocks, buckets))

    hop2[1] = hop(hop1[1], 2)
    swap1[1] = swap(hop1[1])
    relay0 = grid.permute(blocks[0], lambda z, x, y, c: (z, x, 1 - y, c) if c != x else None)
    relay1 = grid.permute(blocks[2], lambda z, x, y, c: (z, 1 - x, y, c) if c == x else None)
    sizes = grid.permute(buckets, lambda z, x, y, c: (z, c, y, x))
    blocks += [relay0, relay1]
    hop3 = [hop(hop2[0], 3), None]
    swap2 = [swap(hop2[0]), None]
    hop2[1], blocks, sizes = lax.optimization_barrier((hop2[1], blocks, sizes))

    hop3[1] = hop(hop2[1], 3)
    swap2[1] = swap(hop2[1])
    act0 = activation(where, sizes, gn_gain, gn_shift, group, blocks, 0, half)
    act1 = activation(where, sizes, gn_gain, gn_shift, group, blocks, half, half)
    acts = [act0, act1]

    def arrived(n, *hops):
        return [value[n] for one in hops for value in one]

    near = (hop1, swap1, hop2, swap2)
    weights = list(pieces) + arrived(0, near) + arrived(1, near)
    main = convolution(main_kernel, where, acts, weights, part, rows, 3)

    hop3, main = lax.optimization_barrier((hop3, main))
    swap3 = [swap(value) for value in hop3]
    far = (hop2, swap2, hop3, swap3)
    last = convolution(
        last_kernel, where, acts, arrived(0, far) + arrived(1, far), part, rows, 1
    )
    bias = time_bias[:, None, :]
    result = main_result(where, buckets, latents, bias, spread(main))
    return last_result(where, buckets, bias, result, spread(last))


def solution(mesh):
    in_specs = (
        P("dp", "space", None, None),
        P("dp", None),
        P(),
        P(),
        P(None, "dp", None),
        P("dp", None),
    )
    grid = Grid(mesh)

    def body(latents, *rest):
        if (grid.Z, grid.Y) == (4, 2) and latents.shape[1] == 2:
            return frame_plan(grid, latents, *rest)
        return row_plan(latents, *rest)

    return jax.shard_map(
        body, mesh=mesh, in_specs=in_specs, out_specs=P("dp", "space", None, None), check_vma=False
    )
```

```python
import functools

import jax
import jax.numpy as jnp
from jax import lax
from jax.experimental import pallas as pl
from jax.experimental.pallas import tpu as pltpu
from jax.sharding import PartitionSpec as P

GROUPS = 32
EPS = 1e-05
FRAME_BYTES = 8 << 20


def with_halo(x, sides, width):
    for axis, dim in sides:
        size, length = (lax.axis_size(axis), x.shape[dim])
        up = [(i, (i + 1) % size) for i in range(size - 1)]
        down = [(j, i) for i, j in up]
        last = lax.slice_in_dim(x, length - width, length, axis=dim)
        first = lax.slice_in_dim(x, 0, width, axis=dim)
        before = lax.ppermute(last, axis, up)
        after = lax.ppermute(first, axis, down)
        x = jnp.concatenate([before, x, after], axis=dim)
    return x


def tap_product(window, panel):
    return lax.dot_general(
        window, panel, (((3,), (1,)), ((), ())), preferred_element_type=jnp.float32
    )


def row_plan(latents, buckets, gn_gain, gn_shift, conv_weight, time_bias):
    frames, rows, cols, chans = latents.shape
    members = chans // GROUPS
    row_ids = lax.axis_index("space") * rows + jnp.arange(rows, dtype=jnp.int32)
    col_ids = jnp.arange(cols, dtype=jnp.int32)
    valid = (
        (row_ids[None, :, None] < buckets[:, 0][:, None, None])
        & (col_ids[None, None, :] < buckets[:, 1][:, None, None])
    ).astype(jnp.float32)
    count = (buckets[:, 0] * buckets[:, 1]).astype(jnp.float32)[:, None] * members
    values = latents.astype(jnp.float32).reshape(frames, rows, cols, GROUPS, members)
    weight_mask = valid[:, :, :, None, None]
    total = lax.psum(jnp.sum(values * weight_mask, axis=(1, 2, 4)), "space")
    mean = total / count
    centered = values - mean[:, None, None, :, None]
    spread = lax.psum(jnp.sum(centered * centered * weight_mask, axis=(1, 2, 4)), "space") / count
    normed = (centered / jnp.sqrt(spread[:, None, None, :, None] + EPS)).reshape(
        frames, rows, cols, chans
    )
    normed = normed * gn_gain + gn_shift
    act = (valid[..., None] * jax.nn.silu(normed)).astype(jnp.bfloat16)
    extended = with_halo(act, (("space", 1),), 1)
    padded = jnp.pad(extended, ((0, 0), (0, 0), (1, 1), (0, 0)))

    def add_tap(index, accum):
        window = lax.dynamic_slice(
            padded, (0, index // 3, index % 3, 0), (frames, rows, cols, chans)
        )
        panel = lax.dynamic_index_in_dim(conv_weight, index, 0, keepdims=False)
        return accum + tap_product(window, lax.all_gather(panel, "dp", axis=0, tiled=True))

    conv = lax.fori_loop(0, 9, add_tap, jnp.zeros((frames, rows, cols, chans), jnp.float32))
    conv_out = conv.astype(jnp.bfloat16)
    summed = latents.astype(jnp.float32) + valid[..., None] * (
        conv_out.astype(jnp.float32) + time_bias[:, None, None, :]
    )
    return summed.astype(jnp.bfloat16)


class Grid:
    def __init__(self, mesh):
        dp, space = mesh.shape["dp"], mesh.shape["space"]
        self.X = self.C = 2
        self.Z, self.Y = dp // 2, space // 2
        self.places = [
            (z, x, y, c)
            for z in range(self.Z)
            for x in range(2)
            for y in range(self.Y)
            for c in range(2)
        ]

    def linear(self, z, x, y, c):
        return ((z * 2 + x) * self.Y + y) * 2 + c

    def permute(self, value, target):
        pairs = []
        for place in self.places:
            goal = target(*place)
            if goal is not None:
                pairs.append((self.linear(*place), self.linear(*goal)))
        return lax.ppermute(value, ("dp", "space"), pairs)


LANES = 128
ANY = pl.BlockSpec(memory_space=pl.ANY)
VMEM = pl.BlockSpec(memory_space=pltpu.VMEM)
SMEM = pl.BlockSpec(memory_space=pltpu.SMEM)


def params(mib):
    return pltpu.CompilerParams(vmem_limit_bytes=mib << 20)


def start_all(pairs, sems):
    copies = [pltpu.make_async_copy(src, dst, sems.at[n]) for n, (src, dst) in enumerate(pairs)]
    for copy in copies:
        copy.start()
    return copies


def piece_kernel(part, where, weight, out, sems):
    rows = pl.ds(pl.multiple_of(where[2] * part, part), part)
    pairs = [(weight.at[tap, rows, :], out.at[tap]) for tap in range(out.shape[0])]
    for copy in start_all(pairs, sems):
        copy.wait()


def own_piece(where, weight, part):
    taps, _, chans = weight.shape
    return pl.pallas_call(
        functools.partial(piece_kernel, part),
        out_shape=jax.ShapeDtypeStruct((taps, part, chans), weight.dtype),
        in_specs=[SMEM, ANY],
        out_specs=VMEM,
        scratch_shapes=[pltpu.SemaphoreType.DMA((taps,))],
        compiler_params=params(56),
        cost_estimate=pl.CostEstimate(flops=0, transcendentals=0, bytes_accessed=4 << 20),
        name="own_piece",
    )(where, weight)


def choose(index, sources, target, sem, wait):
    for value, source in enumerate(sources):

        @pl.when(index == value)
        def _(source=source):
            copy = pltpu.make_async_copy(source, target, sem)
            copy.wait() if wait else copy.start()


def exact_dot(value, ones):
    total = None
    for _ in range(3):
        top = value.astype(jnp.bfloat16)
        term = jnp.dot(top, ones, preferred_element_type=jnp.float32)
        total = term if total is None else total + term
        value = value - top.astype(jnp.float32)
    return total


def per_frame(values, rest):
    ids = lax.broadcasted_iota(jnp.int32, (8, LANES), 0)
    out = jnp.full((8, LANES), rest, jnp.float32)
    for f, value in enumerate(values):
        out = jnp.where(ids == f, value, out)
    return out


def cells_of(sizes, f, first_row, rows):
    held = jnp.clip(sizes[f, 0] - first_row, 0, rows)
    return (held * sizes[f, 1]).astype(jnp.float32)


def stats_kernel(where, sizes, latents, group, group_t, out, sums, scale):
    frames, rows, cols, chans = latents.shape
    members = chans // GROUPS
    first_row = rows * (2 * where[2] + where[3])
    col_ids = lax.broadcasted_iota(jnp.int32, (cols, LANES), 0)

    def add(f, centred):
        masks = [
            col_ids < jnp.where(first_row + r < sizes[f, 0], sizes[f, 1], 0) for r in range(rows)
        ]
        for tile in range(chans // LANES):
            lanes = slice(tile * LANES, (tile + 1) * LANES)
            total = jnp.zeros((8, LANES), jnp.float32)
            for r in range(rows):
                v = latents[f, r, :, lanes].astype(jnp.float32)
                if centred:
                    v = v - scale[f, :, lanes]
                    v = v * v
                v = jnp.where(masks[r], v, 0.0)
                total += jnp.sum(v.reshape(cols // 8, 8, LANES), axis=0)
            sums[f, :, lanes] = total
        return 0

    sums[...] = jnp.zeros_like(sums)
    lax.fori_loop(0, frames, lambda f, _: add(f, False), 0)
    counts = [cells_of(sizes, f, first_row, rows) * members for f in range(frames)]
    count = jnp.maximum(per_frame(counts, 1.0), 1.0)
    mean = exact_dot(jnp.sum(sums[...], axis=1), group[...]) / count
    out[0] = mean
    spread_mean = exact_dot(mean, group_t[...])
    for f in range(frames):
        scale[f] = spread_mean[f : f + 1]
    lax.fori_loop(0, frames, lambda f, _: add(f, True), 0)
    out[1] = exact_dot(jnp.sum(sums[...], axis=1), group[...])


def local_stats(where, sizes, latents, group):
    chans = latents.shape[3]
    return pl.pallas_call(
        stats_kernel,
        out_shape=jax.ShapeDtypeStruct((2, 8, LANES), jnp.float32),
        in_specs=[SMEM, SMEM] + [VMEM] * 3,
        out_specs=VMEM,
        scratch_shapes=[
            pltpu.VMEM((8, 8, chans), jnp.float32),
            pltpu.VMEM((8, 1, chans), jnp.float32),
        ],
        compiler_params=params(4),
        cost_estimate=pl.CostEstimate(
            flops=latents.size // 8, transcendentals=0, bytes_accessed=latents.size // 8
        ),
        name="local_stats",
    )(where, sizes, latents, *group)


def block_rows(where, rows, k):
    return rows * (2 * (where[2] ^ (k // 2)) + (where[1] ^ (k % 2)))


def activate(where, sizes, shift, scale, blocks, act, first_round):
    frames, rows, cols, chans = blocks.shape[1:]
    col_ids = lax.broadcasted_iota(jnp.int32, (cols, LANES), 0)

    def body(f, _):
        for tile in range(chans // LANES):
            lanes = slice(tile * LANES, (tile + 1) * LANES)
            middle = scale[f, :, lanes]
            factor = scale[8 + f, :, lanes]
            offset = shift[:, lanes]
            for n in range(2):
                first = block_rows(where, rows, first_round + n)
                for r in range(rows):
                    limit = jnp.where(first + r < sizes[f, 0], sizes[f, 1], 0)
                    v = blocks[n, f, r, :, lanes].astype(jnp.float32)
                    v = 0.5 * ((v - middle) * factor + offset)
                    v = v + v * jnp.tanh(v)
                    v = jnp.where(col_ids < limit, v, 0.0)
                    act[first + r + 1, f, :, lanes] = v.astype(jnp.bfloat16)
        return 0

    lax.fori_loop(0, frames, body, 0)


def fetch(where, choices, blocks, sems):
    away = jnp.where(where[3] == where[1], 0, 1)
    for wait in (False, True):
        for n, pair in enumerate(choices):
            choose(away, pair, blocks.at[n], sems.at[n], wait)


def first_act_kernel(where, sizes, gain, shift, group, group_t, s0, s1, s2, s3, *refs):
    own, first, sibling, second, act, scale, blocks, sems = refs
    frames, rows, cols, chans = blocks.shape[1:]
    members = chans // GROUPS
    fetch(where, [(own, first), (sibling, second)], blocks, sems)
    whole = per_frame(
        [(sizes[f, 0] * sizes[f, 1] * members).astype(jnp.float32) for f in range(frames)], 1.0
    )
    counts = [
        per_frame(
            [
                cells_of(sizes, f, block_rows(where, rows, k), rows) * members
                for f in range(frames)
            ],
            0.0,
        )
        for k in range(4)
    ]
    stats = (s0, s1, s2, s3)
    mean = sum(count * stat[0] for count, stat in zip(counts, stats)) / whole
    squares = sum(
        stat[1] + count * (stat[0] - mean) * (stat[0] - mean)
        for count, stat in zip(counts, stats)
    )
    factor = exact_dot(1.0 / jnp.sqrt(squares / whole + EPS), group_t[...]) * gain[...]
    middle = exact_dot(mean, group_t[...])
    del group
    for f in range(frames):
        scale[f] = middle[f : f + 1]
        scale[8 + f] = factor[f : f + 1]
    edge = jnp.zeros((frames, cols, chans), jnp.bfloat16)
    act[0] = edge
    act[act.shape[0] - 1] = edge
    activate(where, sizes, shift, scale, blocks, act, 0)


def second_act_kernel(where, sizes, shift, scale, given, *refs):
    first, relay0, second, relay1, act, blocks, sems = refs
    del given
    fetch(where, [(first, relay0), (second, relay1)], blocks, sems)
    activate(where, sizes, shift, scale, blocks, act, 2)


def act_params(frames, rows, cols, chans):
    elements = 2 * frames * rows * cols * chans
    return dict(
        compiler_params=params(16),
        cost_estimate=pl.CostEstimate(
            flops=elements // 8, transcendentals=0, bytes_accessed=elements // 8
        ),
    )


def first_activation(where, sizes, gain, shift, group, stats, blocks):
    frames, rows, cols, chans = blocks[0].shape
    return pl.pallas_call(
        first_act_kernel,
        out_shape=[
            jax.ShapeDtypeStruct((4 * rows + 2, frames, cols, chans), jnp.bfloat16),
            jax.ShapeDtypeStruct((16, 1, chans), jnp.float32),
        ],
        in_specs=[SMEM, SMEM] + [VMEM] * 8 + [ANY] * 4,
        out_specs=[VMEM] * 2,
        scratch_shapes=[
            pltpu.VMEM((2, frames, rows, cols, chans), jnp.bfloat16),
            pltpu.SemaphoreType.DMA((2,)),
        ],
        name="first_activation",
        **act_params(frames, rows, cols, chans),
    )(where, sizes, gain[None, :], shift[None, :], *group, *stats, *blocks)


def second_activation(where, sizes, shift, scale, act, blocks):
    frames, rows, cols, chans = blocks[0].shape
    return pl.pallas_call(
        second_act_kernel,
        out_shape=jax.ShapeDtypeStruct(act.shape, act.dtype),
        in_specs=[SMEM, SMEM] + [VMEM] * 3 + [ANY] * 4,
        out_specs=VMEM,
        scratch_shapes=[
            pltpu.VMEM((2, frames, rows, cols, chans), jnp.bfloat16),
            pltpu.SemaphoreType.DMA((2,)),
        ],
        input_output_aliases={4: 0},
        name="second_activation",
        **act_params(frames, rows, cols, chans),
    )(where, sizes, shift[None, :], scale, act, *blocks)


def group_matrix(chans):
    member = jnp.arange(chans, dtype=jnp.int32)[:, None] // (chans // GROUPS)
    return (member == jnp.arange(LANES, dtype=jnp.int32)[None, :]).astype(jnp.bfloat16)


def shifted_sum(left, middle, right, cols):
    size = middle.shape[0]
    col = lax.broadcasted_iota(jnp.int32, middle.shape, 0) % cols
    left = jnp.where(col == 0, 0.0, pltpu.roll(left, 1, 0))
    right = jnp.where(col == cols - 1, 0.0, pltpu.roll(right, size - 1, 0))
    return middle + left + right


def window(act, base, dr, chunk, line, cols):
    return act[pl.ds(pl.multiple_of(base + dr * line, cols), chunk), :]


def product(rows, weight):
    return lax.dot_general(
        rows, weight, (((1,), (1,)), ((), ())), preferred_element_type=jnp.float32
    )


def give_rows(where, result, outs, rows):
    width = result.shape[3]
    for k, out in enumerate(outs):
        out[:, :, :, 0:width] = result[pl.ds(block_rows(where, rows, k), rows)]
        if out.shape[3] > width:
            blank = out.shape[:3] + (out.shape[3] - width,)
            out[:, :, :, width:] = jnp.zeros(blank, out.dtype)


def all_rows(act, result, cols, compute):
    height, frames = result.shape[:2]
    line = frames * cols
    chunk = height * line // 2
    lines = chunk // line

    def body(m, _):
        base = pl.multiple_of(m * chunk, chunk)
        value = compute(act, base, chunk, line).astype(jnp.bfloat16)
        result[pl.ds(m * lines, lines)] = value.reshape(lines, frames, cols, value.shape[1])
        return 0

    lax.fori_loop(0, 2, body, 0)


def from_below(hop, c):
    return 2 * hop + c


def from_above(hop, c):
    return 2 * hop + 1 - c


def main_kernel(rows, cols, part, where, act, *refs):
    z, c = where[0], where[3]
    own, hops, refs = refs[0], refs[1:5], refs[5:]
    outs, weight, result, sems = refs[:4], *refs[4:]
    low = jnp.where(z < 2, 0, 1)

    def rows_of(place):
        return pl.ds(pl.multiple_of(place * part, part), part)

    first = jnp.where(z == 0, from_above(0, c), from_below(0, c))
    second = jnp.where(
        z == 0, from_above(1, c), jnp.where(z == 3, from_below(1, c), from_above(0, c))
    )
    first_rows = rows_of(jnp.where(z == 0, 1, z - 1) - low)
    second_rows = rows_of(jnp.where(z < 3, 2, 0))
    for wait in (False, True):
        choose(0, (own,), weight.at[:, rows_of(z - low), :], sems.at[0], wait)
        choose(first, hops[:2], weight.at[:, first_rows, :], sems.at[1], wait)
        choose(second, hops, weight.at[:, second_rows, :], sems.at[2], wait)

    def compute(act, base, chunk, line):
        columns = []
        for dc in range(3):
            total = None
            for dr in range(3):
                term = product(window(act, base, dr, chunk, line, cols), weight[3 * dr + dc])
                total = term if total is None else total + term
            columns.append(total)
        return shifted_sum(*columns, cols)

    all_rows(act, result, cols, compute)
    give_rows(where, result, outs, rows)


def farthest(where):
    z, c = where[0], where[3]
    return jnp.where(
        z < 2,
        jnp.where(z == 0, from_above(1, c), from_above(0, c)),
        jnp.where(z == 2, from_below(0, c), from_below(1, c)),
    )


def tap_rows(act, weight, part, base, chunk, line, cols, first):
    total = None
    for n in range(weight.shape[0] // 3):
        taps = weight[3 * n : 3 * n + 3].reshape(3 * part, weight.shape[2])
        term = product(window(act, base, first + n, chunk, line, cols), taps)
        total = term if total is None else total + term
    return total


def last_kernel(rows, cols, part, where, act, *refs):
    hops, refs = refs[:4], refs[4:]
    outs, weight, result, sems = refs[:4], *refs[4:]
    for wait in (False, True):
        choose(farthest(where), hops, weight, sems.at[0], wait)

    def compute(act, base, chunk, line):
        total = tap_rows(act, weight, part, base, chunk, line, cols, 0)
        columns = [total[:, dc * part : (dc + 1) * part] for dc in range(3)]
        return shifted_sum(*columns, cols)

    all_rows(act, result, cols, compute)
    give_rows(where, result, outs, rows)


def convolution(kernel, where, act, weights, part, rows, shards):
    padded, frames, cols, chans = act.shape
    height = padded - 2
    taps, width = 9, part * shards
    lanes = -(-width // LANES) * LANES
    out = jax.ShapeDtypeStruct((rows, frames, cols, lanes), jnp.bfloat16)
    return pl.pallas_call(
        functools.partial(kernel, rows, cols, part),
        out_shape=[out] * 4,
        in_specs=[SMEM, VMEM] + [ANY] * len(weights),
        out_specs=[VMEM] * 4,
        scratch_shapes=[
            pltpu.VMEM((taps, width, chans), jnp.bfloat16),
            pltpu.VMEM((height, frames, cols, width), jnp.bfloat16),
            pltpu.SemaphoreType.DMA((3,)),
        ],
        compiler_params=params(24),
        cost_estimate=pl.CostEstimate(
            flops=height * frames * cols, transcendentals=0, bytes_accessed=width * chans
        ),
        name="convolution",
    )(where, act.reshape(padded * frames * cols, chans), *weights)


def place_of(where, k):
    return 2 * (where[3] ^ (k % 2)) + (where[2] ^ (k // 2))


def bring(where, parts, buffer, sems):
    copies = [
        pltpu.make_async_copy(part, buffer.at[place_of(where, k)], sems.at[k])
        for k, part in enumerate(parts)
    ]
    for copy in copies:
        copy.start()
    for copy in copies:
        copy.wait()


def window_of(low, chans):
    quarter = chans // 4
    wide = -(-quarter // LANES) * LANES
    if low:
        return slice(0, wide), slice(0, quarter)
    return slice(chans - wide, chans), slice(wide - quarter, wide)


def main_result_kernel(where, sizes, latents, bias, *refs):
    parts, out, slab, buffer, sems = refs[:4], *refs[4:]
    frames, rows, cols, chans = latents.shape
    part = chans // 16
    bring(where, parts, buffer, sems)
    first_row = rows * (2 * where[2] + where[3])
    col_ids = lax.broadcasted_iota(jnp.int32, (cols, 12 * part), 0)

    def finish(low):
        lanes = slice(low * 4 * part, (low + 3) * 4 * part)
        rest = slice(12 * part, chans) if low == 0 else slice(0, 4 * part)
        view, _ = window_of(low, chans)

        def body(f, _):
            for r in range(rows):
                chunks = [
                    buffer[q, r, f, :, n * part : (n + 1) * part].astype(jnp.float32)
                    for n in range(3)
                    for q in range(4)
                ]
                value = jnp.concatenate(chunks, axis=1) + bias[f, :, lanes]
                limit = jnp.where(first_row + r < sizes[f, 0], sizes[f, 1], 0)
                value = jnp.where(col_ids < limit, value, 0.0)
                value += latents[f, r, :, lanes].astype(jnp.float32)
                out[f, r, :, lanes] = value.astype(jnp.bfloat16)
                out[f, r, :, rest] = latents[f, r, :, rest]
                slab[f, r] = out[f, r, :, view]
            return 0

        lax.fori_loop(0, frames, body, 0)

    for low in (0, 1):
        pl.when((where[0] >= 2) == bool(low))(functools.partial(finish, low))


def main_result(where, sizes, latents, bias, parts):
    frames, rows, cols, chans = latents.shape
    view, _ = window_of(1, chans)
    return pl.pallas_call(
        main_result_kernel,
        out_shape=[
            jax.ShapeDtypeStruct(latents.shape, latents.dtype),
            jax.ShapeDtypeStruct((frames, rows, cols, view.stop), latents.dtype),
        ],
        in_specs=[SMEM, SMEM, VMEM, VMEM] + [ANY] * 4,
        out_specs=[VMEM] * 2,
        scratch_shapes=[
            pltpu.VMEM((4,) + parts[0].shape, jnp.bfloat16),
            pltpu.SemaphoreType.DMA((4,)),
        ],
        compiler_params=params(12),
        cost_estimate=pl.CostEstimate(
            flops=latents.size // 8, transcendentals=0, bytes_accessed=latents.size // 8
        ),
        name="main_result",
    )(where, sizes, latents, bias, *parts)


def last_result_kernel(where, sizes, bias, slab, p0, p1, p2, p3, given, out, done, sems):
    del given
    frames, rows, cols, wide = slab.shape
    chans = out.shape[3]
    part = chans // 16
    y, c = where[2], where[3]
    first_row = rows * (2 * y + c)
    col_ids = lax.broadcasted_iota(jnp.int32, (cols, 4 * part), 0)

    def part_of(q, f, r):
        pieces = [ref[r, f, :, 0:part].astype(jnp.float32) for ref in (p0, p1, p2, p3)]
        near = [pieces[0], pieces[1]] if q // 2 == 0 else [pieces[1], pieces[0]]
        other = [pieces[2], pieces[3]] if q // 2 == 0 else [pieces[3], pieces[2]]
        pair = [jnp.where(c == 0, *near), jnp.where(c == 0, *other)]
        return jnp.where(y == q % 2, pair[0], pair[1])

    def finish(low):
        view, inner = window_of(low, chans)
        lanes = slice(0, 4 * part) if low else slice(chans - 4 * part, chans)
        copies = []
        for f in range(frames):
            for r in range(rows):
                value = jnp.concatenate([part_of(q, f, r) for q in range(4)], axis=1)
                value = value + bias[f, :, lanes]
                limit = jnp.where(first_row + r < sizes[f, 0], sizes[f, 1], 0)
                value = jnp.where(col_ids < limit, value, 0.0)
                value += slab[f, r, :, inner].astype(jnp.float32)
                done[f, r] = slab[f, r]
                done[f, r, :, inner] = value.astype(jnp.bfloat16)
            copies.append(
                pltpu.make_async_copy(done.at[f], out.at[f, :, :, view], sems.at[f])
            )
            copies[-1].start()
        for copy in copies:
            copy.wait()

    for low in (0, 1):
        pl.when((where[0] >= 2) == bool(low))(functools.partial(finish, low))


def last_result(where, sizes, bias, given, slab, parts):
    return pl.pallas_call(
        last_result_kernel,
        out_shape=jax.ShapeDtypeStruct(given.shape, given.dtype),
        in_specs=[SMEM, SMEM, VMEM, VMEM] + [VMEM] * 4 + [ANY],
        out_specs=ANY,
        scratch_shapes=[
            pltpu.VMEM(slab.shape, slab.dtype),
            pltpu.SemaphoreType.DMA((slab.shape[0],)),
        ],
        input_output_aliases={8: 0},
        compiler_params=params(4),
        cost_estimate=pl.CostEstimate(
            flops=given.size, transcendentals=0, bytes_accessed=given.size
        ),
        name="last_result",
    )(where, sizes, bias, slab, *parts, given)


def frame_plan(grid, latents, buckets, gn_gain, gn_shift, conv_weight, time_bias):
    frames, rows, cols, chans = latents.shape
    part = conv_weight.shape[1] // 2
    dp_index, space_index = lax.axis_index("dp"), lax.axis_index("space")
    z, x = dp_index // 2, dp_index % 2
    y, c = space_index // 2, space_index % 2
    where = jnp.stack([z, x, y, c]).astype(jnp.int32)

    def spread(values):
        return [
            grid.permute(v, lambda z, x, y, c, k=k: (z, c, y ^ (k // 2), x ^ (k % 2)))
            for k, v in enumerate(values)
        ]

    def hop(value, step):
        def target(z, x, y, c):
            if c == 0:
                return (z + 1, x, y, c) if step - 1 <= z < 3 else None
            return (z - 1, x, y, c) if 1 <= z <= 4 - step else None

        return grid.permute(value, target)

    def swap(value):
        return grid.permute(value, lambda z, x, y, c: (z, x, y, 1 - c))

    group = group_matrix(chans)
    group = (group, group.T)

    piece = own_piece(where, conv_weight, part)
    hop1 = hop(piece, 1)
    first = grid.permute(
        latents, lambda z, x, y, c: (z, x, 1 - y, c) if c == x else (z, 1 - x, y, 1 - c)
    )
    second = grid.permute(
        latents, lambda z, x, y, c: (z, 1 - x, y, c) if c == x else (z, x, 1 - y, 1 - c)
    )
    sibling = grid.permute(latents, lambda z, x, y, c: (z, x, y, 1 - c) if c != x else None)
    stats = local_stats(where, buckets, latents, group)
    stats = [
        grid.permute(stats, lambda z, x, y, c, k=k: (z, c ^ (k % 2), y ^ (k // 2), x))
        for k in range(4)
    ]
    sizes = grid.permute(buckets, lambda z, x, y, c: (z, c, y, x))
    hop1, first, sibling, stats, sizes = lax.optimization_barrier(
        (hop1, first, sibling, stats, sizes)
    )

    hop2 = hop(hop1, 2)
    swap1 = swap(hop1)
    relay0 = grid.permute(first, lambda z, x, y, c: (z, x, 1 - y, c) if c != x else None)
    relay1 = grid.permute(first, lambda z, x, y, c: (z, 1 - x, y, c) if c == x else None)
    act, scale = first_activation(
        where, sizes, gn_gain, gn_shift, group, stats, [latents, first, sibling, second]
    )
    hop2, relay0, relay1, act = lax.optimization_barrier((hop2, relay0, relay1, act))

    hop3 = hop(hop2, 3)
    swap2 = swap(hop2)
    act = second_activation(
        where, sizes, gn_shift, scale, act, [first, relay0, second, relay1]
    )
    near = [hop1, swap1, hop2, swap2]
    main = convolution(main_kernel, where, act, [piece] + near, part, rows, 3)

    main = spread(main)
    hop3, main[0] = lax.optimization_barrier((hop3, main[0]))
    swap3 = swap(hop3)
    last = convolution(last_kernel, where, act, [hop2, swap2, hop3, swap3], part, rows, 1)
    bias = time_bias[:, None, :]
    result, slab = main_result(where, buckets, latents, bias, main)
    return last_result(where, buckets, bias, result, slab, spread(last))


def solution(mesh):
    in_specs = (
        P("dp", "space", None, None),
        P("dp", None),
        P(),
        P(),
        P(None, "dp", None),
        P("dp", None),
    )
    grid = Grid(mesh)

    def body(latents, *rest):
        if (grid.Z, grid.Y) == (4, 2) and latents.shape[1] == 2:
            return frame_plan(grid, latents, *rest)
        return row_plan(latents, *rest)

    return jax.shard_map(
        body, mesh=mesh, in_specs=in_specs, out_specs=P("dp", "space", None, None), check_vma=False
    )
```

```python
import functools

import jax
import jax.numpy as jnp
from jax import lax
from jax.experimental import pallas as pl
from jax.experimental.pallas import tpu as pltpu
from jax.sharding import PartitionSpec as P

GROUPS = 32
EPS = 1e-05
FRAME_BYTES = 8 << 20


def with_halo(x, sides, width):
    for axis, dim in sides:
        size, length = (lax.axis_size(axis), x.shape[dim])
        up = [(i, (i + 1) % size) for i in range(size - 1)]
        down = [(j, i) for i, j in up]
        last = lax.slice_in_dim(x, length - width, length, axis=dim)
        first = lax.slice_in_dim(x, 0, width, axis=dim)
        before = lax.ppermute(last, axis, up)
        after = lax.ppermute(first, axis, down)
        x = jnp.concatenate([before, x, after], axis=dim)
    return x


def tap_product(window, panel):
    return lax.dot_general(
        window, panel, (((3,), (1,)), ((), ())), preferred_element_type=jnp.float32
    )


def row_plan(latents, buckets, gn_gain, gn_shift, conv_weight, time_bias):
    frames, rows, cols, chans = latents.shape
    members = chans // GROUPS
    row_ids = lax.axis_index("space") * rows + jnp.arange(rows, dtype=jnp.int32)
    col_ids = jnp.arange(cols, dtype=jnp.int32)
    valid = (
        (row_ids[None, :, None] < buckets[:, 0][:, None, None])
        & (col_ids[None, None, :] < buckets[:, 1][:, None, None])
    ).astype(jnp.float32)
    count = (buckets[:, 0] * buckets[:, 1]).astype(jnp.float32)[:, None] * members
    values = latents.astype(jnp.float32).reshape(frames, rows, cols, GROUPS, members)
    weight_mask = valid[:, :, :, None, None]
    total = lax.psum(jnp.sum(values * weight_mask, axis=(1, 2, 4)), "space")
    mean = total / count
    centered = values - mean[:, None, None, :, None]
    spread = lax.psum(jnp.sum(centered * centered * weight_mask, axis=(1, 2, 4)), "space") / count
    normed = (centered / jnp.sqrt(spread[:, None, None, :, None] + EPS)).reshape(
        frames, rows, cols, chans
    )
    normed = normed * gn_gain + gn_shift
    act = (valid[..., None] * jax.nn.silu(normed)).astype(jnp.bfloat16)
    extended = with_halo(act, (("space", 1),), 1)
    padded = jnp.pad(extended, ((0, 0), (0, 0), (1, 1), (0, 0)))

    def add_tap(index, accum):
        window = lax.dynamic_slice(
            padded, (0, index // 3, index % 3, 0), (frames, rows, cols, chans)
        )
        panel = lax.dynamic_index_in_dim(conv_weight, index, 0, keepdims=False)
        return accum + tap_product(window, lax.all_gather(panel, "dp", axis=0, tiled=True))

    conv = lax.fori_loop(0, 9, add_tap, jnp.zeros((frames, rows, cols, chans), jnp.float32))
    conv_out = conv.astype(jnp.bfloat16)
    summed = latents.astype(jnp.float32) + valid[..., None] * (
        conv_out.astype(jnp.float32) + time_bias[:, None, None, :]
    )
    return summed.astype(jnp.bfloat16)


class Grid:
    def __init__(self, mesh):
        dp, space = mesh.shape["dp"], mesh.shape["space"]
        self.X = self.C = 2
        self.Z, self.Y = dp // 2, space // 2
        self.places = [
            (z, x, y, c)
            for z in range(self.Z)
            for x in range(2)
            for y in range(self.Y)
            for c in range(2)
        ]

    def linear(self, z, x, y, c):
        return ((z * 2 + x) * self.Y + y) * 2 + c

    def permute(self, value, target):
        pairs = []
        for place in self.places:
            goal = target(*place)
            if goal is not None:
                pairs.append((self.linear(*place), self.linear(*goal)))
        return lax.ppermute(value, ("dp", "space"), pairs)


LANES = 128
ANY = pl.BlockSpec(memory_space=pl.ANY)
VMEM = pl.BlockSpec(memory_space=pltpu.VMEM)
SMEM = pl.BlockSpec(memory_space=pltpu.SMEM)


def params(mib):
    return pltpu.CompilerParams(vmem_limit_bytes=mib << 20)


def start_all(pairs, sems):
    copies = [pltpu.make_async_copy(src, dst, sems.at[n]) for n, (src, dst) in enumerate(pairs)]
    for copy in copies:
        copy.start()
    return copies


def piece_kernel(part, weight, out, sems):
    y = lax.axis_index("space") // 2
    rows = pl.ds(pl.multiple_of(y * part, part), part)
    pairs = [(weight.at[tap, rows, :], out.at[tap]) for tap in range(out.shape[0])]
    for copy in start_all(pairs, sems):
        copy.wait()


def own_piece(weight, part):
    taps, _, chans = weight.shape
    return pl.pallas_call(
        functools.partial(piece_kernel, part),
        out_shape=jax.ShapeDtypeStruct((taps, part, chans), weight.dtype),
        in_specs=[ANY],
        out_specs=VMEM,
        scratch_shapes=[pltpu.SemaphoreType.DMA((taps,))],
        compiler_params=params(56),
        cost_estimate=pl.CostEstimate(flops=0, transcendentals=0, bytes_accessed=4 << 20),
        name="own_piece",
    )(weight)


def choose(index, sources, target, sem, wait):
    for value, source in enumerate(sources):

        @pl.when(index == value)
        def _(source=source):
            copy = pltpu.make_async_copy(source, target, sem)
            copy.wait() if wait else copy.start()


def exact_dot(value, ones):
    total = None
    for _ in range(3):
        top = value.astype(jnp.bfloat16)
        term = jnp.dot(top, ones, preferred_element_type=jnp.float32)
        total = term if total is None else total + term
        value = value - top.astype(jnp.float32)
    return total


def per_frame(values, rest):
    ids = lax.broadcasted_iota(jnp.int32, (8, LANES), 0)
    out = jnp.full((8, LANES), rest, jnp.float32)
    for f, value in enumerate(values):
        out = jnp.where(ids == f, value, out)
    return out


def cells_of(sizes, f, first_row, rows):
    held = jnp.clip(sizes[f, 0] - first_row, 0, rows)
    return (held * sizes[f, 1]).astype(jnp.float32)


def block_rows(where, rows, k):
    return rows * (2 * (where[2] ^ (k // 2)) + (where[1] ^ (k % 2)))


def fetch(where, choices, blocks, sems):
    away = jnp.where(where[3] == where[1], 0, 1)
    for wait in (False, True):
        for n, pair in enumerate(choices):
            choose(away, pair, blocks.at[n], sems.at[n], wait)


def cells_in(where, sizes, rounds, frames, rows, members, rest):
    return per_frame(
        [
            sum(cells_of(sizes, f, block_rows(where, rows, k), rows) for k in rounds) * members
            for f in range(frames)
        ],
        rest,
    )


def reduce_blocks(where, sizes, blocks, rounds, group, group_t, sums, scale):
    frames, rows, cols, chans = blocks.shape[1:]
    members = chans // GROUPS
    col_ids = lax.broadcasted_iota(jnp.int32, (cols, LANES), 0)
    first_rows = [block_rows(where, rows, k) for k in rounds]

    def add(f, centred):
        places = [(k, r, first + r) for k, first in zip(rounds, first_rows) for r in range(rows)]
        masks = [col_ids < jnp.where(row < sizes[f, 0], sizes[f, 1], 0) for _, _, row in places]
        for tile in range(chans // LANES):
            lanes = slice(tile * LANES, (tile + 1) * LANES)
            total = jnp.zeros((8, LANES), jnp.float32)
            for (k, r, _), mask in zip(places, masks):
                v = blocks[k, f, r, :, lanes].astype(jnp.float32)
                if centred:
                    v = v - scale[f, :, lanes]
                    v = v * v
                v = jnp.where(mask, v, 0.0)
                total += jnp.sum(v.reshape(cols // 8, 8, LANES), axis=0)
            sums[f, :, lanes] = total
        return 0

    sums[...] = jnp.zeros_like(sums)
    lax.fori_loop(0, frames, lambda f, _: add(f, False), 0)
    count = jnp.maximum(cells_in(where, sizes, rounds, frames, rows, members, 1.0), 1.0)
    mean = exact_dot(jnp.sum(sums[...], axis=1), group[...]) / count
    wide = exact_dot(mean, group_t[...])
    for f in range(frames):
        scale[f] = wide[f : f + 1]
    lax.fori_loop(0, frames, lambda f, _: add(f, True), 0)
    return mean, exact_dot(jnp.sum(sums[...], axis=1), group[...])


def stats_kernel(where, sizes, group, group_t, own, first, sibling, second, *refs):
    out, blocks, sums, scale, sems = refs
    fetch(where, [(own, first), (sibling, second)], blocks, sems)
    mean, squares = reduce_blocks(where, sizes, blocks, (0, 1), group, group_t, sums, scale)
    out[0] = mean
    out[1] = squares


def act_kernel(where, sizes, gain, shift, group, group_t, stats, *refs):
    own, first, sibling, second, relay0, relay1, act, blocks, sums, scale, sems = refs
    frames, rows, cols, chans = blocks.shape[1:]
    members = chans // GROUPS
    fetch(
        where,
        [(own, first), (sibling, second), (first, relay0), (second, relay1)],
        blocks,
        sems,
    )
    mean1, squares1 = reduce_blocks(where, sizes, blocks, (2, 3), group, group_t, sums, scale)
    mean0, squares0 = stats[0], stats[1]
    count0 = cells_in(where, sizes, (0, 1), frames, rows, members, 0.0)
    count1 = cells_in(where, sizes, (2, 3), frames, rows, members, 0.0)
    whole = jnp.maximum(count0 + count1, 1.0)
    mean = (count0 * mean0 + count1 * mean1) / whole
    squares = squares0 + squares1
    squares += count0 * (mean0 - mean) * (mean0 - mean)
    squares += count1 * (mean1 - mean) * (mean1 - mean)
    factor = exact_dot(1.0 / jnp.sqrt(squares / whole + EPS), group_t[...]) * gain[...]
    middle = exact_dot(mean, group_t[...])
    for f in range(frames):
        scale[f] = middle[f : f + 1]
        scale[8 + f] = factor[f : f + 1]
    edge = jnp.zeros((frames, cols, chans), jnp.bfloat16)
    act[0] = edge
    act[act.shape[0] - 1] = edge
    col_ids = lax.broadcasted_iota(jnp.int32, (cols, LANES), 0)
    first_rows = [block_rows(where, rows, k) for k in range(4)]

    def body(f, _):
        for tile in range(chans // LANES):
            lanes = slice(tile * LANES, (tile + 1) * LANES)
            middle = scale[f, :, lanes]
            factor = scale[8 + f, :, lanes]
            offset = shift[:, lanes]
            for k in range(4):
                for r in range(rows):
                    row = first_rows[k] + r
                    limit = jnp.where(row < sizes[f, 0], sizes[f, 1], 0)
                    v = blocks[k, f, r, :, lanes].astype(jnp.float32)
                    v = 0.5 * ((v - middle) * factor + offset)
                    v = v + v * jnp.tanh(v)
                    v = jnp.where(col_ids < limit, v, 0.0)
                    act[row + 1, f, :, lanes] = v.astype(jnp.bfloat16)
        return 0

    lax.fori_loop(0, frames, body, 0)


def act_params(count, frames, rows, cols, chans):
    elements = frames * rows * cols * chans
    return dict(
        scratch_shapes=[
            pltpu.VMEM((count, frames, rows, cols, chans), jnp.bfloat16),
            pltpu.VMEM((8, 8, chans), jnp.float32),
            pltpu.VMEM((16, 1, chans), jnp.float32),
            pltpu.SemaphoreType.DMA((count,)),
        ],
        compiler_params=params(16),
        cost_estimate=pl.CostEstimate(
            flops=elements // 8, transcendentals=0, bytes_accessed=elements // 8
        ),
    )


def early_stats(where, sizes, group, blocks):
    return pl.pallas_call(
        stats_kernel,
        out_shape=jax.ShapeDtypeStruct((2, 8, LANES), jnp.float32),
        in_specs=[SMEM, SMEM] + [VMEM] * 2 + [ANY] * 4,
        out_specs=VMEM,
        name="early_stats",
        **act_params(2, *blocks[0].shape),
    )(where, sizes, *group, *blocks)


def activation(where, sizes, gain, shift, group, stats, blocks):
    frames, rows, cols, chans = blocks[0].shape
    return pl.pallas_call(
        act_kernel,
        out_shape=jax.ShapeDtypeStruct((4 * rows + 2, frames, cols, chans), jnp.bfloat16),
        in_specs=[SMEM, SMEM] + [VMEM] * 5 + [ANY] * 6,
        out_specs=VMEM,
        name="activation",
        **act_params(4, frames, rows, cols, chans),
    )(where, sizes, gain[None, :], shift[None, :], *group, stats, *blocks)


def group_matrix(chans):
    member = jnp.arange(chans, dtype=jnp.int32)[:, None] // (chans // GROUPS)
    return (member == jnp.arange(LANES, dtype=jnp.int32)[None, :]).astype(jnp.bfloat16)


def shifted_sum(left, middle, right, cols):
    size = middle.shape[0]
    col = lax.broadcasted_iota(jnp.int32, middle.shape, 0) % cols
    left = jnp.where(col == 0, 0.0, pltpu.roll(left, 1, 0))
    right = jnp.where(col == cols - 1, 0.0, pltpu.roll(right, size - 1, 0))
    return middle + left + right


def window(act, base, dr, chunk, line, cols):
    return act[pl.ds(pl.multiple_of(base + dr * line, cols), chunk), :]


def product(rows, weight):
    return lax.dot_general(
        rows, weight, (((1,), (1,)), ((), ())), preferred_element_type=jnp.float32
    )


def give_rows(where, result, outs, rows):
    width = result.shape[3]
    for k, out in enumerate(outs):
        out[:, :, :, 0:width] = result[pl.ds(block_rows(where, rows, k), rows)]
        if out.shape[3] > width:
            blank = out.shape[:3] + (out.shape[3] - width,)
            out[:, :, :, width:] = jnp.zeros(blank, out.dtype)


def all_rows(act, result, cols, compute):
    height, frames = result.shape[:2]
    line = frames * cols
    chunk = height * line // 2
    lines = chunk // line

    def body(m, _):
        base = pl.multiple_of(m * chunk, chunk)
        value = compute(act, base, chunk, line).astype(jnp.bfloat16)
        result[pl.ds(m * lines, lines)] = value.reshape(lines, frames, cols, value.shape[1])
        return 0

    lax.fori_loop(0, 2, body, 0)


def from_below(hop, c):
    return 2 * hop + c


def from_above(hop, c):
    return 2 * hop + 1 - c


def main_kernel(rows, cols, part, where, act, *refs):
    z, c = where[0], where[3]
    own, hops, refs = refs[0], refs[1:5], refs[5:]
    outs, weight, result, sems = refs[:4], *refs[4:]
    low = jnp.where(z < 2, 0, 1)

    def rows_of(place):
        return pl.ds(pl.multiple_of(place * part, part), part)

    first = jnp.where(z == 0, from_above(0, c), from_below(0, c))
    second = jnp.where(
        z == 0, from_above(1, c), jnp.where(z == 3, from_below(1, c), from_above(0, c))
    )
    first_rows = rows_of(jnp.where(z == 0, 1, z - 1) - low)
    second_rows = rows_of(jnp.where(z < 3, 2, 0))
    for wait in (False, True):
        choose(0, (own,), weight.at[:, rows_of(z - low), :], sems.at[0], wait)
        choose(first, hops[:2], weight.at[:, first_rows, :], sems.at[1], wait)
        choose(second, hops, weight.at[:, second_rows, :], sems.at[2], wait)

    def compute(act, base, chunk, line):
        columns = []
        for dc in range(3):
            total = None
            for dr in range(3):
                term = product(window(act, base, dr, chunk, line, cols), weight[3 * dr + dc])
                total = term if total is None else total + term
            columns.append(total)
        return shifted_sum(*columns, cols)

    all_rows(act, result, cols, compute)
    give_rows(where, result, outs, rows)


def farthest(where):
    z, c = where[0], where[3]
    return jnp.where(
        z < 2,
        jnp.where(z == 0, from_above(1, c), from_above(0, c)),
        jnp.where(z == 2, from_below(0, c), from_below(1, c)),
    )


def tap_rows(act, weight, part, base, chunk, line, cols, first):
    total = None
    for n in range(weight.shape[0] // 3):
        taps = weight[3 * n : 3 * n + 3].reshape(3 * part, weight.shape[2])
        term = product(window(act, base, first + n, chunk, line, cols), taps)
        total = term if total is None else total + term
    return total


def last_kernel(rows, cols, part, where, act, *refs):
    hops, refs = refs[:4], refs[4:]
    outs, weight, result, sems = refs[:4], *refs[4:]
    for wait in (False, True):
        choose(farthest(where), hops, weight, sems.at[0], wait)

    def compute(act, base, chunk, line):
        total = tap_rows(act, weight, part, base, chunk, line, cols, 0)
        columns = [total[:, dc * part : (dc + 1) * part] for dc in range(3)]
        return shifted_sum(*columns, cols)

    all_rows(act, result, cols, compute)
    give_rows(where, result, outs, rows)


def convolution(kernel, where, act, weights, part, rows, shards):
    padded, frames, cols, chans = act.shape
    height = padded - 2
    taps, width = 9, part * shards
    lanes = -(-width // LANES) * LANES
    out = jax.ShapeDtypeStruct((rows, frames, cols, lanes), jnp.bfloat16)
    return pl.pallas_call(
        functools.partial(kernel, rows, cols, part),
        out_shape=[out] * 4,
        in_specs=[SMEM, VMEM] + [ANY] * len(weights),
        out_specs=[VMEM] * 4,
        scratch_shapes=[
            pltpu.VMEM((taps, width, chans), jnp.bfloat16),
            pltpu.VMEM((height, frames, cols, width), jnp.bfloat16),
            pltpu.SemaphoreType.DMA((3,)),
        ],
        compiler_params=params(24),
        cost_estimate=pl.CostEstimate(
            flops=height * frames * cols, transcendentals=0, bytes_accessed=width * chans
        ),
        name="convolution",
    )(where, act.reshape(padded * frames * cols, chans), *weights)


def place_of(where, k):
    return 2 * (where[3] ^ (k % 2)) + (where[2] ^ (k // 2))


def bring(where, parts, buffer, sems):
    copies = [
        pltpu.make_async_copy(part, buffer.at[place_of(where, k)], sems.at[k])
        for k, part in enumerate(parts)
    ]
    for copy in copies:
        copy.start()
    for copy in copies:
        copy.wait()


def window_of(low, chans):
    quarter = chans // 4
    wide = -(-quarter // LANES) * LANES
    if low:
        return slice(0, wide), slice(0, quarter)
    return slice(chans - wide, chans), slice(wide - quarter, wide)


def main_result_kernel(where, sizes, latents, bias, *refs):
    parts, out, slab, buffer, sems = refs[:4], *refs[4:]
    frames, rows, cols, chans = latents.shape
    part = chans // 16
    bring(where, parts, buffer, sems)
    first_row = rows * (2 * where[2] + where[3])
    col_ids = lax.broadcasted_iota(jnp.int32, (cols, 12 * part), 0)

    def finish(low):
        lanes = slice(low * 4 * part, (low + 3) * 4 * part)
        rest = slice(12 * part, chans) if low == 0 else slice(0, 4 * part)
        view, _ = window_of(low, chans)

        def body(f, _):
            for r in range(rows):
                chunks = [
                    buffer[q, r, f, :, n * part : (n + 1) * part].astype(jnp.float32)
                    for n in range(3)
                    for q in range(4)
                ]
                value = jnp.concatenate(chunks, axis=1) + bias[f, :, lanes]
                limit = jnp.where(first_row + r < sizes[f, 0], sizes[f, 1], 0)
                value = jnp.where(col_ids < limit, value, 0.0)
                value += latents[f, r, :, lanes].astype(jnp.float32)
                out[f, r, :, lanes] = value.astype(jnp.bfloat16)
                out[f, r, :, rest] = latents[f, r, :, rest]
                slab[f, r] = out[f, r, :, view]
            return 0

        lax.fori_loop(0, frames, body, 0)

    for low in (0, 1):
        pl.when((where[0] >= 2) == bool(low))(functools.partial(finish, low))


def main_result(where, sizes, latents, bias, parts):
    frames, rows, cols, chans = latents.shape
    view, _ = window_of(1, chans)
    return pl.pallas_call(
        main_result_kernel,
        out_shape=[
            jax.ShapeDtypeStruct(latents.shape, latents.dtype),
            jax.ShapeDtypeStruct((frames, rows, cols, view.stop), latents.dtype),
        ],
        in_specs=[SMEM, SMEM, VMEM, VMEM] + [ANY] * 4,
        out_specs=[VMEM] * 2,
        scratch_shapes=[
            pltpu.VMEM((4,) + parts[0].shape, jnp.bfloat16),
            pltpu.SemaphoreType.DMA((4,)),
        ],
        compiler_params=params(12),
        cost_estimate=pl.CostEstimate(
            flops=latents.size // 8, transcendentals=0, bytes_accessed=latents.size // 8
        ),
        name="main_result",
    )(where, sizes, latents, bias, *parts)


def last_result_kernel(where, sizes, bias, slab, p0, p1, p2, p3, given, out, done, sems):
    del given
    frames, rows, cols, wide = slab.shape
    chans = out.shape[3]
    part = chans // 16
    y, c = where[2], where[3]
    first_row = rows * (2 * y + c)
    col_ids = lax.broadcasted_iota(jnp.int32, (cols, 4 * part), 0)

    def part_of(q, f, r):
        pieces = [ref[r, f, :, 0:part].astype(jnp.float32) for ref in (p0, p1, p2, p3)]
        near = [pieces[0], pieces[1]] if q // 2 == 0 else [pieces[1], pieces[0]]
        other = [pieces[2], pieces[3]] if q // 2 == 0 else [pieces[3], pieces[2]]
        pair = [jnp.where(c == 0, *near), jnp.where(c == 0, *other)]
        return jnp.where(y == q % 2, pair[0], pair[1])

    def finish(low):
        view, inner = window_of(low, chans)
        lanes = slice(0, 4 * part) if low else slice(chans - 4 * part, chans)
        copies = []
        for f in range(frames):
            for r in range(rows):
                value = jnp.concatenate([part_of(q, f, r) for q in range(4)], axis=1)
                value = value + bias[f, :, lanes]
                limit = jnp.where(first_row + r < sizes[f, 0], sizes[f, 1], 0)
                value = jnp.where(col_ids < limit, value, 0.0)
                value += slab[f, r, :, inner].astype(jnp.float32)
                done[f, r] = slab[f, r]
                done[f, r, :, inner] = value.astype(jnp.bfloat16)
            copies.append(
                pltpu.make_async_copy(done.at[f], out.at[f, :, :, view], sems.at[f])
            )
            copies[-1].start()
        for copy in copies:
            copy.wait()

    for low in (0, 1):
        pl.when((where[0] >= 2) == bool(low))(functools.partial(finish, low))


def last_result(where, sizes, bias, given, slab, parts):
    return pl.pallas_call(
        last_result_kernel,
        out_shape=jax.ShapeDtypeStruct(given.shape, given.dtype),
        in_specs=[SMEM, SMEM, VMEM, VMEM] + [VMEM] * 4 + [ANY],
        out_specs=ANY,
        scratch_shapes=[
            pltpu.VMEM(slab.shape, slab.dtype),
            pltpu.SemaphoreType.DMA((slab.shape[0],)),
        ],
        input_output_aliases={8: 0},
        compiler_params=params(4),
        cost_estimate=pl.CostEstimate(
            flops=given.size, transcendentals=0, bytes_accessed=given.size
        ),
        name="last_result",
    )(where, sizes, bias, slab, *parts, given)


def frame_plan(grid, latents, buckets, gn_gain, gn_shift, conv_weight, time_bias):
    frames, rows, cols, chans = latents.shape
    part = conv_weight.shape[1] // 2
    dp_index, space_index = lax.axis_index("dp"), lax.axis_index("space")
    z, x = dp_index // 2, dp_index % 2
    y, c = space_index // 2, space_index % 2
    where = jnp.stack([z, x, y, c]).astype(jnp.int32)

    def spread(values):
        return [
            grid.permute(v, lambda z, x, y, c, k=k: (z, c, y ^ (k // 2), x ^ (k % 2)))
            for k, v in enumerate(values)
        ]

    def hop(value, step):
        def target(z, x, y, c):
            if c == 0:
                return (z + 1, x, y, c) if step - 1 <= z < 3 else None
            return (z - 1, x, y, c) if 1 <= z <= 4 - step else None

        return grid.permute(value, target)

    def swap(value):
        return grid.permute(value, lambda z, x, y, c: (z, x, y, 1 - c))

    group = group_matrix(chans)
    group = (group, group.T)

    piece = own_piece(conv_weight, part)
    hop1 = hop(piece, 1)
    first = grid.permute(
        latents, lambda z, x, y, c: (z, x, 1 - y, c) if c == x else (z, 1 - x, y, 1 - c)
    )
    second = grid.permute(
        latents, lambda z, x, y, c: (z, 1 - x, y, c) if c == x else (z, x, 1 - y, 1 - c)
    )
    sibling = grid.permute(latents, lambda z, x, y, c: (z, x, y, 1 - c) if c != x else None)
    sizes = grid.permute(buckets, lambda z, x, y, c: (z, c, y, x))

    hop2 = hop(hop1, 2)
    first, second, sibling, sizes = lax.optimization_barrier((first, second, sibling, sizes))
    relay0 = grid.permute(first, lambda z, x, y, c: (z, x, 1 - y, c) if c != x else None)
    relay1 = grid.permute(first, lambda z, x, y, c: (z, 1 - x, y, c) if c == x else None)
    blocks = [latents, first, sibling, second]
    stats = early_stats(where, sizes, group, blocks)
    swap1 = swap(hop1)
    hop2, relay0, relay1, stats, swap1 = lax.optimization_barrier(
        (hop2, relay0, relay1, stats, swap1)
    )

    hop3 = hop(hop2, 3)
    swap2 = swap(hop2)
    blocks += [relay0, relay1]
    act = activation(where, sizes, gn_gain, gn_shift, group, stats, blocks)
    near = [hop1, swap1, hop2, swap2]
    main = convolution(main_kernel, where, act, [piece] + near, part, rows, 3)

    hop3, main = lax.optimization_barrier((hop3, main))
    main = spread(main)
    swap3 = swap(hop3)
    last = convolution(last_kernel, where, act, [hop2, swap2, hop3, swap3], part, rows, 1)
    bias = time_bias[:, None, :]
    result, slab = main_result(where, buckets, latents, bias, main)
    return last_result(where, buckets, bias, result, slab, spread(last))


def solution(mesh):
    in_specs = (
        P("dp", "space", None, None),
        P("dp", None),
        P(),
        P(),
        P(None, "dp", None),
        P("dp", None),
    )
    grid = Grid(mesh)

    def body(latents, *rest):
        if (grid.Z, grid.Y) == (4, 2) and latents.shape[1] == 2:
            return frame_plan(grid, latents, *rest)
        return row_plan(latents, *rest)

    return jax.shard_map(
        body, mesh=mesh, in_specs=in_specs, out_specs=P("dp", "space", None, None), check_vma=False
    )
```

```python
import functools

import jax
import jax.numpy as jnp
from jax import lax
from jax.experimental import pallas as pl
from jax.experimental.pallas import tpu as pltpu
from jax.sharding import PartitionSpec as P

GROUPS = 32
EPS = 1e-05
FRAME_BYTES = 8 << 20


def with_halo(x, sides, width):
    for axis, dim in sides:
        size, length = (lax.axis_size(axis), x.shape[dim])
        up = [(i, (i + 1) % size) for i in range(size - 1)]
        down = [(j, i) for i, j in up]
        last = lax.slice_in_dim(x, length - width, length, axis=dim)
        first = lax.slice_in_dim(x, 0, width, axis=dim)
        before = lax.ppermute(last, axis, up)
        after = lax.ppermute(first, axis, down)
        x = jnp.concatenate([before, x, after], axis=dim)
    return x


def tap_product(window, panel):
    return lax.dot_general(
        window, panel, (((3,), (1,)), ((), ())), preferred_element_type=jnp.float32
    )


def row_plan(latents, buckets, gn_gain, gn_shift, conv_weight, time_bias):
    frames, rows, cols, chans = latents.shape
    members = chans // GROUPS
    row_ids = lax.axis_index("space") * rows + jnp.arange(rows, dtype=jnp.int32)
    col_ids = jnp.arange(cols, dtype=jnp.int32)
    valid = (
        (row_ids[None, :, None] < buckets[:, 0][:, None, None])
        & (col_ids[None, None, :] < buckets[:, 1][:, None, None])
    ).astype(jnp.float32)
    count = (buckets[:, 0] * buckets[:, 1]).astype(jnp.float32)[:, None] * members
    values = latents.astype(jnp.float32).reshape(frames, rows, cols, GROUPS, members)
    weight_mask = valid[:, :, :, None, None]
    total = lax.psum(jnp.sum(values * weight_mask, axis=(1, 2, 4)), "space")
    mean = total / count
    centered = values - mean[:, None, None, :, None]
    spread = lax.psum(jnp.sum(centered * centered * weight_mask, axis=(1, 2, 4)), "space") / count
    normed = (centered / jnp.sqrt(spread[:, None, None, :, None] + EPS)).reshape(
        frames, rows, cols, chans
    )
    normed = normed * gn_gain + gn_shift
    act = (valid[..., None] * jax.nn.silu(normed)).astype(jnp.bfloat16)
    extended = with_halo(act, (("space", 1),), 1)
    padded = jnp.pad(extended, ((0, 0), (0, 0), (1, 1), (0, 0)))

    def add_tap(index, accum):
        window = lax.dynamic_slice(
            padded, (0, index // 3, index % 3, 0), (frames, rows, cols, chans)
        )
        panel = lax.dynamic_index_in_dim(conv_weight, index, 0, keepdims=False)
        return accum + tap_product(window, lax.all_gather(panel, "dp", axis=0, tiled=True))

    conv = lax.fori_loop(0, 9, add_tap, jnp.zeros((frames, rows, cols, chans), jnp.float32))
    conv_out = conv.astype(jnp.bfloat16)
    summed = latents.astype(jnp.float32) + valid[..., None] * (
        conv_out.astype(jnp.float32) + time_bias[:, None, None, :]
    )
    return summed.astype(jnp.bfloat16)


class Grid:
    def __init__(self, mesh):
        dp, space = mesh.shape["dp"], mesh.shape["space"]
        self.X = self.C = 2
        self.Z, self.Y = dp // 2, space // 2
        self.places = [
            (z, x, y, c)
            for z in range(self.Z)
            for x in range(2)
            for y in range(self.Y)
            for c in range(2)
        ]

    def linear(self, z, x, y, c):
        return ((z * 2 + x) * self.Y + y) * 2 + c

    def permute(self, value, target):
        pairs = []
        for place in self.places:
            goal = target(*place)
            if goal is not None:
                pairs.append((self.linear(*place), self.linear(*goal)))
        return lax.ppermute(value, ("dp", "space"), pairs)


LANES = 128
ANY = pl.BlockSpec(memory_space=pl.ANY)
VMEM = pl.BlockSpec(memory_space=pltpu.VMEM)
SMEM = pl.BlockSpec(memory_space=pltpu.SMEM)


def params(mib):
    return pltpu.CompilerParams(vmem_limit_bytes=mib << 20)


def start_all(pairs, sems):
    copies = [pltpu.make_async_copy(src, dst, sems.at[n]) for n, (src, dst) in enumerate(pairs)]
    for copy in copies:
        copy.start()
    return copies


def piece_kernel(part, weight, out, sems):
    y = lax.axis_index("space") // 2
    rows = pl.ds(pl.multiple_of(y * part, part), part)
    pairs = [(weight.at[tap, rows, :], out.at[tap]) for tap in range(out.shape[0])]
    for copy in start_all(pairs, sems):
        copy.wait()


def own_piece(weight, part):
    taps, _, chans = weight.shape
    return pl.pallas_call(
        functools.partial(piece_kernel, part),
        out_shape=jax.ShapeDtypeStruct((taps, part, chans), weight.dtype),
        in_specs=[ANY],
        out_specs=VMEM,
        scratch_shapes=[pltpu.SemaphoreType.DMA((taps,))],
        compiler_params=params(56),
        cost_estimate=pl.CostEstimate(flops=0, transcendentals=0, bytes_accessed=4 << 20),
        name="own_piece",
    )(weight)


def choose(index, sources, target, sem, wait):
    for value, source in enumerate(sources):

        @pl.when(index == value)
        def _(source=source):
            copy = pltpu.make_async_copy(source, target, sem)
            copy.wait() if wait else copy.start()


def exact_dot(value, ones):
    total = None
    for _ in range(3):
        top = value.astype(jnp.bfloat16)
        term = jnp.dot(top, ones, preferred_element_type=jnp.float32)
        total = term if total is None else total + term
        value = value - top.astype(jnp.float32)
    return total


def per_frame(values, rest):
    ids = lax.broadcasted_iota(jnp.int32, (8, LANES), 0)
    out = jnp.full((8, LANES), rest, jnp.float32)
    for f, value in enumerate(values):
        out = jnp.where(ids == f, value, out)
    return out


def cells_of(sizes, f, first_row, rows):
    held = jnp.clip(sizes[f, 0] - first_row, 0, rows)
    return (held * sizes[f, 1]).astype(jnp.float32)


def block_rows(where, rows, k):
    return rows * (2 * (where[2] ^ (k // 2)) + (where[1] ^ (k % 2)))


def fetch(where, choices, blocks, sems):
    away = jnp.where(where[3] == where[1], 0, 1)
    for wait in (False, True):
        for n, pair in enumerate(choices):
            choose(away, pair, blocks.at[n], sems.at[n], wait)


def cells_in(where, sizes, rounds, frames, rows, members, rest):
    return per_frame(
        [
            sum(cells_of(sizes, f, block_rows(where, rows, k), rows) for k in rounds) * members
            for f in range(frames)
        ],
        rest,
    )


def reduce_blocks(where, sizes, blocks, rounds, group, group_t, sums, scale):
    frames, rows, cols, chans = blocks.shape[1:]
    members = chans // GROUPS
    col_ids = lax.broadcasted_iota(jnp.int32, (cols, LANES), 0)
    first_rows = [block_rows(where, rows, k) for k in rounds]

    def add(f, centred):
        places = [(k, r, first + r) for k, first in zip(rounds, first_rows) for r in range(rows)]
        masks = [col_ids < jnp.where(row < sizes[f, 0], sizes[f, 1], 0) for _, _, row in places]
        for tile in range(chans // LANES):
            lanes = slice(tile * LANES, (tile + 1) * LANES)
            total = jnp.zeros((8, LANES), jnp.float32)
            for (k, r, _), mask in zip(places, masks):
                v = blocks[k, f, r, :, lanes].astype(jnp.float32)
                if centred:
                    v = v - scale[f, :, lanes]
                    v = v * v
                v = jnp.where(mask, v, 0.0)
                total += jnp.sum(v.reshape(cols // 8, 8, LANES), axis=0)
            sums[f, :, lanes] = total
        return 0

    sums[...] = jnp.zeros_like(sums)
    lax.fori_loop(0, frames, lambda f, _: add(f, False), 0)
    count = jnp.maximum(cells_in(where, sizes, rounds, frames, rows, members, 1.0), 1.0)
    mean = exact_dot(jnp.sum(sums[...], axis=1), group[...]) / count
    wide = exact_dot(mean, group_t[...])
    for f in range(frames):
        scale[f] = wide[f : f + 1]
    lax.fori_loop(0, frames, lambda f, _: add(f, True), 0)
    return mean, exact_dot(jnp.sum(sums[...], axis=1), group[...])


def stats_kernel(where, sizes, group, group_t, own, first, sibling, second, *refs):
    out, blocks, sums, scale, sems = refs
    fetch(where, [(own, first), (sibling, second)], blocks, sems)
    mean, squares = reduce_blocks(where, sizes, blocks, (0, 1), group, group_t, sums, scale)
    out[0] = mean
    out[1] = squares


def act_kernel(where, sizes, gain, shift, group, group_t, stats, *refs):
    own, first, sibling, second, relay0, relay1, act, blocks, sums, scale, sems = refs
    frames, rows, cols, chans = blocks.shape[1:]
    members = chans // GROUPS
    away = jnp.where(where[3] == where[1], 0, 1)
    choices = [(own, first), (sibling, second), (first, relay0), (second, relay1)]

    def bring_block(k, wait):
        choose(away, choices[k], blocks.at[k], sems.at[k], wait)

    for k in (2, 3, 0, 1):
        bring_block(k, False)
    for k in (2, 3):
        bring_block(k, True)
    mean1, squares1 = reduce_blocks(where, sizes, blocks, (2, 3), group, group_t, sums, scale)
    for k in (0, 1):
        bring_block(k, True)
    mean0, squares0 = stats[0], stats[1]
    count0 = cells_in(where, sizes, (0, 1), frames, rows, members, 0.0)
    count1 = cells_in(where, sizes, (2, 3), frames, rows, members, 0.0)
    whole = jnp.maximum(count0 + count1, 1.0)
    mean = (count0 * mean0 + count1 * mean1) / whole
    squares = squares0 + squares1
    squares += count0 * (mean0 - mean) * (mean0 - mean)
    squares += count1 * (mean1 - mean) * (mean1 - mean)
    factor = exact_dot(1.0 / jnp.sqrt(squares / whole + EPS), group_t[...]) * gain[...]
    middle = exact_dot(mean, group_t[...])
    for f in range(frames):
        scale[f] = middle[f : f + 1]
        scale[8 + f] = factor[f : f + 1]
    edge = jnp.zeros((frames, cols, chans), jnp.bfloat16)
    act[0] = edge
    act[act.shape[0] - 1] = edge
    col_ids = lax.broadcasted_iota(jnp.int32, (cols, LANES), 0)
    first_rows = [block_rows(where, rows, k) for k in range(4)]

    def body(f, _):
        for tile in range(chans // LANES):
            lanes = slice(tile * LANES, (tile + 1) * LANES)
            middle = scale[f, :, lanes]
            factor = scale[8 + f, :, lanes]
            offset = shift[:, lanes]
            for k in range(4):
                for r in range(rows):
                    row = first_rows[k] + r
                    limit = jnp.where(row < sizes[f, 0], sizes[f, 1], 0)
                    v = blocks[k, f, r, :, lanes].astype(jnp.float32)
                    v = 0.5 * ((v - middle) * factor + offset)
                    v = v + v * jnp.tanh(v)
                    v = jnp.where(col_ids < limit, v, 0.0)
                    act[row + 1, f, :, lanes] = v.astype(jnp.bfloat16)
        return 0

    lax.fori_loop(0, frames, body, 0)


def act_params(count, frames, rows, cols, chans):
    elements = frames * rows * cols * chans
    return dict(
        scratch_shapes=[
            pltpu.VMEM((count, frames, rows, cols, chans), jnp.bfloat16),
            pltpu.VMEM((8, 8, chans), jnp.float32),
            pltpu.VMEM((16, 1, chans), jnp.float32),
            pltpu.SemaphoreType.DMA((count,)),
        ],
        compiler_params=params(16),
        cost_estimate=pl.CostEstimate(
            flops=elements // 8, transcendentals=0, bytes_accessed=elements // 8
        ),
    )


def early_stats(where, sizes, group, blocks):
    return pl.pallas_call(
        stats_kernel,
        out_shape=jax.ShapeDtypeStruct((2, 8, LANES), jnp.float32),
        in_specs=[SMEM, SMEM] + [VMEM] * 2 + [ANY] * 4,
        out_specs=VMEM,
        name="early_stats",
        **act_params(2, *blocks[0].shape),
    )(where, sizes, *group, *blocks)


def activation(where, sizes, gain, shift, group, stats, blocks):
    frames, rows, cols, chans = blocks[0].shape
    return pl.pallas_call(
        act_kernel,
        out_shape=jax.ShapeDtypeStruct((4 * rows + 2, frames, cols, chans), jnp.bfloat16),
        in_specs=[SMEM, SMEM] + [VMEM] * 5 + [ANY] * 6,
        out_specs=VMEM,
        name="activation",
        **act_params(4, frames, rows, cols, chans),
    )(where, sizes, gain[None, :], shift[None, :], *group, stats, *blocks)


def group_matrix(chans):
    member = jnp.arange(chans, dtype=jnp.int32)[:, None] // (chans // GROUPS)
    return (member == jnp.arange(LANES, dtype=jnp.int32)[None, :]).astype(jnp.bfloat16)


def shifted_sum(left, middle, right, cols):
    size = middle.shape[0]
    col = lax.broadcasted_iota(jnp.int32, middle.shape, 0) % cols
    left = jnp.where(col == 0, 0.0, pltpu.roll(left, 1, 0))
    right = jnp.where(col == cols - 1, 0.0, pltpu.roll(right, size - 1, 0))
    return middle + left + right


def window(act, base, dr, chunk, line, cols):
    return act[pl.ds(pl.multiple_of(base + dr * line, cols), chunk), :]


def product(rows, weight):
    return lax.dot_general(
        rows, weight, (((1,), (1,)), ((), ())), preferred_element_type=jnp.float32
    )


def give_rows(where, result, outs, rows):
    width = result.shape[3]
    for k, out in enumerate(outs):
        out[:, :, :, 0:width] = result[pl.ds(block_rows(where, rows, k), rows)]
        if out.shape[3] > width:
            blank = out.shape[:3] + (out.shape[3] - width,)
            out[:, :, :, width:] = jnp.zeros(blank, out.dtype)


def all_rows(act, result, cols, compute):
    height, frames = result.shape[:2]
    line = frames * cols
    chunk = height * line
    lines = chunk // line

    def body(m, _):
        base = pl.multiple_of(m * chunk, chunk)
        value = compute(act, base, chunk, line).astype(jnp.bfloat16)
        result[pl.ds(m * lines, lines)] = value.reshape(lines, frames, cols, value.shape[1])
        return 0

    lax.fori_loop(0, 1, body, 0)


def from_below(hop, c):
    return 2 * hop + c


def from_above(hop, c):
    return 2 * hop + 1 - c


def main_kernel(rows, cols, part, where, act, *refs):
    z, c = where[0], where[3]
    own, hops, refs = refs[0], refs[1:5], refs[5:]
    outs, weight, result, sems = refs[:4], *refs[4:]
    low = jnp.where(z < 2, 0, 1)

    def rows_of(place):
        return pl.ds(pl.multiple_of(place * part, part), part)

    first = jnp.where(z == 0, from_above(0, c), from_below(0, c))
    second = jnp.where(
        z == 0, from_above(1, c), jnp.where(z == 3, from_below(1, c), from_above(0, c))
    )
    first_rows = rows_of(jnp.where(z == 0, 1, z - 1) - low)
    second_rows = rows_of(jnp.where(z < 3, 2, 0))
    for wait in (False, True):
        choose(0, (own,), weight.at[:, rows_of(z - low), :], sems.at[0], wait)
        choose(first, hops[:2], weight.at[:, first_rows, :], sems.at[1], wait)
        choose(second, hops, weight.at[:, second_rows, :], sems.at[2], wait)

    def compute(act, base, chunk, line):
        columns = []
        for dc in range(3):
            total = None
            for dr in range(3):
                term = product(window(act, base, dr, chunk, line, cols), weight[3 * dr + dc])
                total = term if total is None else total + term
            columns.append(total)
        return shifted_sum(*columns, cols)

    all_rows(act, result, cols, compute)
    give_rows(where, result, outs, rows)


def farthest(where):
    z, c = where[0], where[3]
    return jnp.where(
        z < 2,
        jnp.where(z == 0, from_above(1, c), from_above(0, c)),
        jnp.where(z == 2, from_below(0, c), from_below(1, c)),
    )


def tap_rows(act, weight, part, base, chunk, line, cols, first):
    total = None
    for n in range(weight.shape[0] // 3):
        taps = weight[3 * n : 3 * n + 3].reshape(3 * part, weight.shape[2])
        term = product(window(act, base, first + n, chunk, line, cols), taps)
        total = term if total is None else total + term
    return total


def last_kernel(rows, cols, part, where, act, *refs):
    hops, refs = refs[:4], refs[4:]
    outs, weight, result, sems = refs[:4], *refs[4:]
    for wait in (False, True):
        choose(farthest(where), hops, weight, sems.at[0], wait)

    def compute(act, base, chunk, line):
        total = tap_rows(act, weight, part, base, chunk, line, cols, 0)
        columns = [total[:, dc * part : (dc + 1) * part] for dc in range(3)]
        return shifted_sum(*columns, cols)

    all_rows(act, result, cols, compute)
    give_rows(where, result, outs, rows)


def convolution(kernel, where, act, weights, part, rows, shards):
    padded, frames, cols, chans = act.shape
    height = padded - 2
    taps, width = 9, part * shards
    lanes = -(-width // LANES) * LANES
    out = jax.ShapeDtypeStruct((rows, frames, cols, lanes), jnp.bfloat16)
    return pl.pallas_call(
        functools.partial(kernel, rows, cols, part),
        out_shape=[out] * 4,
        in_specs=[SMEM, VMEM] + [ANY] * len(weights),
        out_specs=[VMEM] * 4,
        scratch_shapes=[
            pltpu.VMEM((taps, width, chans), jnp.bfloat16),
            pltpu.VMEM((height, frames, cols, width), jnp.bfloat16),
            pltpu.SemaphoreType.DMA((3,)),
        ],
        compiler_params=params(24),
        cost_estimate=pl.CostEstimate(
            flops=height * frames * cols, transcendentals=0, bytes_accessed=width * chans
        ),
        name="convolution",
    )(where, act.reshape(padded * frames * cols, chans), *weights)


def place_of(where, k):
    return 2 * (where[3] ^ (k % 2)) + (where[2] ^ (k // 2))


def bring(where, parts, buffer, sems):
    copies = [
        pltpu.make_async_copy(part, buffer.at[place_of(where, k)], sems.at[k])
        for k, part in enumerate(parts)
    ]
    for copy in copies:
        copy.start()
    for copy in copies:
        copy.wait()


def window_of(low, chans):
    quarter = chans // 4
    wide = -(-quarter // LANES) * LANES
    if low:
        return slice(0, wide), slice(0, quarter)
    return slice(chans - wide, chans), slice(wide - quarter, wide)


def main_result_kernel(where, sizes, latents, bias, *refs):
    parts, out, slab, buffer, sems = refs[:4], *refs[4:]
    frames, rows, cols, chans = latents.shape
    part = chans // 16
    bring(where, parts, buffer, sems)
    first_row = rows * (2 * where[2] + where[3])
    col_ids = lax.broadcasted_iota(jnp.int32, (cols, 12 * part), 0)

    def finish(low):
        lanes = slice(low * 4 * part, (low + 3) * 4 * part)
        rest = slice(12 * part, chans) if low == 0 else slice(0, 4 * part)
        view, _ = window_of(low, chans)

        def body(f, _):
            for r in range(rows):
                chunks = [
                    buffer[q, r, f, :, n * part : (n + 1) * part].astype(jnp.float32)
                    for n in range(3)
                    for q in range(4)
                ]
                value = jnp.concatenate(chunks, axis=1) + bias[f, :, lanes]
                limit = jnp.where(first_row + r < sizes[f, 0], sizes[f, 1], 0)
                value = jnp.where(col_ids < limit, value, 0.0)
                value += latents[f, r, :, lanes].astype(jnp.float32)
                out[f, r, :, lanes] = value.astype(jnp.bfloat16)
                out[f, r, :, rest] = latents[f, r, :, rest]
                slab[f, r] = out[f, r, :, view]
            return 0

        lax.fori_loop(0, frames, body, 0)

    for low in (0, 1):
        pl.when((where[0] >= 2) == bool(low))(functools.partial(finish, low))


def main_result(where, sizes, latents, bias, parts):
    frames, rows, cols, chans = latents.shape
    view, _ = window_of(1, chans)
    return pl.pallas_call(
        main_result_kernel,
        out_shape=[
            jax.ShapeDtypeStruct(latents.shape, latents.dtype),
            jax.ShapeDtypeStruct((frames, rows, cols, view.stop), latents.dtype),
        ],
        in_specs=[SMEM, SMEM, VMEM, VMEM] + [ANY] * 4,
        out_specs=[VMEM] * 2,
        scratch_shapes=[
            pltpu.VMEM((4,) + parts[0].shape, jnp.bfloat16),
            pltpu.SemaphoreType.DMA((4,)),
        ],
        compiler_params=params(12),
        cost_estimate=pl.CostEstimate(
            flops=latents.size // 8, transcendentals=0, bytes_accessed=latents.size // 8
        ),
        name="main_result",
    )(where, sizes, latents, bias, *parts)


def last_result_kernel(where, sizes, bias, slab, p0, p1, p2, p3, given, out, done, sems):
    del given
    frames, rows, cols, wide = slab.shape
    chans = out.shape[3]
    part = chans // 16
    y, c = where[2], where[3]
    first_row = rows * (2 * y + c)
    col_ids = lax.broadcasted_iota(jnp.int32, (cols, 4 * part), 0)

    def part_of(q, f, r):
        pieces = [ref[r, f, :, 0:part].astype(jnp.float32) for ref in (p0, p1, p2, p3)]
        near = [pieces[0], pieces[1]] if q // 2 == 0 else [pieces[1], pieces[0]]
        other = [pieces[2], pieces[3]] if q // 2 == 0 else [pieces[3], pieces[2]]
        pair = [jnp.where(c == 0, *near), jnp.where(c == 0, *other)]
        return jnp.where(y == q % 2, pair[0], pair[1])

    def finish(low):
        view, inner = window_of(low, chans)
        lanes = slice(0, 4 * part) if low else slice(chans - 4 * part, chans)
        copies = []
        for f in range(frames):
            for r in range(rows):
                value = jnp.concatenate([part_of(q, f, r) for q in range(4)], axis=1)
                value = value + bias[f, :, lanes]
                limit = jnp.where(first_row + r < sizes[f, 0], sizes[f, 1], 0)
                value = jnp.where(col_ids < limit, value, 0.0)
                value += slab[f, r, :, inner].astype(jnp.float32)
                done[f, r] = slab[f, r]
                done[f, r, :, inner] = value.astype(jnp.bfloat16)
            copies.append(
                pltpu.make_async_copy(done.at[f], out.at[f, :, :, view], sems.at[f])
            )
            copies[-1].start()
        for copy in copies:
            copy.wait()

    for low in (0, 1):
        pl.when((where[0] >= 2) == bool(low))(functools.partial(finish, low))


def last_result(where, sizes, bias, given, slab, parts):
    return pl.pallas_call(
        last_result_kernel,
        out_shape=jax.ShapeDtypeStruct(given.shape, given.dtype),
        in_specs=[SMEM, SMEM, VMEM, VMEM] + [VMEM] * 4 + [ANY],
        out_specs=ANY,
        scratch_shapes=[
            pltpu.VMEM(slab.shape, slab.dtype),
            pltpu.SemaphoreType.DMA((slab.shape[0],)),
        ],
        input_output_aliases={8: 0},
        compiler_params=params(4),
        cost_estimate=pl.CostEstimate(
            flops=given.size, transcendentals=0, bytes_accessed=given.size
        ),
        name="last_result",
    )(where, sizes, bias, slab, *parts, given)


def frame_plan(grid, latents, buckets, gn_gain, gn_shift, conv_weight, time_bias):
    frames, rows, cols, chans = latents.shape
    part = conv_weight.shape[1] // 2
    dp_index, space_index = lax.axis_index("dp"), lax.axis_index("space")
    z, x = dp_index // 2, dp_index % 2
    y, c = space_index // 2, space_index % 2
    where = jnp.stack([z, x, y, c]).astype(jnp.int32)

    def spread(values):
        return [
            grid.permute(v, lambda z, x, y, c, k=k: (z, c, y ^ (k // 2), x ^ (k % 2)))
            for k, v in enumerate(values)
        ]

    def hop(value, step):
        def target(z, x, y, c):
            if c == 0:
                return (z + 1, x, y, c) if step - 1 <= z < 3 else None
            return (z - 1, x, y, c) if 1 <= z <= 4 - step else None

        return grid.permute(value, target)

    def swap(value):
        return grid.permute(value, lambda z, x, y, c: (z, x, y, 1 - c))

    group = group_matrix(chans)
    group = (group, group.T)

    piece = own_piece(conv_weight, part)
    hop1 = hop(piece, 1)
    first = grid.permute(
        latents, lambda z, x, y, c: (z, x, 1 - y, c) if c == x else (z, 1 - x, y, 1 - c)
    )
    second = grid.permute(
        latents, lambda z, x, y, c: (z, 1 - x, y, c) if c == x else (z, x, 1 - y, 1 - c)
    )
    sibling = grid.permute(latents, lambda z, x, y, c: (z, x, y, 1 - c) if c != x else None)
    sizes = grid.permute(buckets, lambda z, x, y, c: (z, c, y, x))

    hop2 = hop(hop1, 2)
    first, second, sibling, sizes = lax.optimization_barrier((first, second, sibling, sizes))
    relay0 = grid.permute(first, lambda z, x, y, c: (z, x, 1 - y, c) if c != x else None)
    relay1 = grid.permute(first, lambda z, x, y, c: (z, 1 - x, y, c) if c == x else None)
    blocks = [latents, first, sibling, second]
    stats = early_stats(where, sizes, group, blocks)
    swap1 = swap(hop1)
    hop2, relay0, relay1, stats, swap1 = lax.optimization_barrier(
        (hop2, relay0, relay1, stats, swap1)
    )

    hop3 = hop(hop2, 3)
    swap2 = swap(hop2)
    blocks += [relay0, relay1]
    act = activation(where, sizes, gn_gain, gn_shift, group, stats, blocks)
    near = [hop1, swap1, hop2, swap2]
    main = convolution(main_kernel, where, act, [piece] + near, part, rows, 3)

    hop3, main = lax.optimization_barrier((hop3, main))
    main = spread(main)
    swap3 = swap(hop3)
    last = convolution(last_kernel, where, act, [hop2, swap2, hop3, swap3], part, rows, 1)
    bias = time_bias[:, None, :]
    result, slab = main_result(where, buckets, latents, bias, main)
    return last_result(where, buckets, bias, result, slab, spread(last))


def solution(mesh):
    in_specs = (
        P("dp", "space", None, None),
        P("dp", None),
        P(),
        P(),
        P(None, "dp", None),
        P("dp", None),
    )
    grid = Grid(mesh)

    def body(latents, *rest):
        if (grid.Z, grid.Y) == (4, 2) and latents.shape[1] == 2:
            return frame_plan(grid, latents, *rest)
        return row_plan(latents, *rest)

    return jax.shard_map(
        body, mesh=mesh, in_specs=in_specs, out_specs=P("dp", "space", None, None), check_vma=False
    )
```
